32 devices in a mesh: groups: 2 (over y), img: 4 (over z), head: 2 (over x), rep: 2 (over core).
Axes of the slice: x: 2, y: 2, z: 4, core: 2. Of those that a mesh axis runs over, the one named last changes fastest.
Arguments:
- enc: bfloat16 [32, 576, 1024], P(('groups', 'img'), 'head'), parts along dimension 0, may hold values from -6 to 6
- pair_list: int32 [32, 2], P('groups'), parts along dimension 0, may hold values from 0 to 15, as said below
- w_embed: bfloat16 [1024, 768], P('rep'), may hold values from -0.1875 to 0.1875
- w_query: bfloat16 [768, 768], P('rep'), may hold values from -0.375 to 0.375
- w_key: bfloat16 [768, 768], P('rep'), may hold values from -0.375 to 0.375
- w_value: bfloat16 [768, 768], P('rep'), may hold values from -0.21875 to 0.21875
- w_out: bfloat16 [768, 768], P('rep'), may hold values from -0.4375 to 0.4375
- w_head: bfloat16 [768, 28], replicated, may hold values from -0.21875 to 0.21875
- gain_query: float32 [768], replicated, may hold values from 0.1 to 1.9
- gain_key: float32 [768], replicated, may hold values from 0.1 to 1.9
Outputs:
- joined: float32 [32, 27, 576], P(('groups', 'img'), None, ('head', 'rep')), parts along dimension 0
The draws below stay inside these ranges and needn't reach their ends.
There are 2 independent parts, one for each index of `groups`. The reference program is written for one: setup_inputs(seed, part) draws one part's arguments, and reference() takes and returns one part's arrays. A program takes and returns all parts, laid end to end along the dimension named above; an argument that names none is the same for every part. Nothing has to cross between parts.
Inputs may be any that keep to these rules, and one draw needn't show every extreme that they name: `pair_list`: pair p is held by the device with img index p // 4, head index p // 2 % 2 and rep index p % 2. Image i is owned by img index i // 4. Among the 4 images named by the pairs of the devices that share an img index and a rep index, no img index owns more than 1, and one owns exactly 1. The two images of a pair have different owners.
All inputs are finite; a program needn't handle non-finite values.
Results may differ from the reference program's by a relative error of at most 0.0085.
Values may be sent and summed in bfloat16 or wider, within the bound.
A program may use at most 64 MiB of HBM per device.

```python
import jax
import jax.numpy as jnp
from jax import lax

D_ENC = 1024
D = 768
HEADS = 12
HEAD_DIM = 64
TOK = 576
IMG_DEV = 4
NIMG = 16
NPAIR = 16
CHANNELS = 28
N_IMG = 4
N_HEAD = 2
N_REP = 2


def permute_owners(group_key):
    return jax.random.permutation(group_key, N_IMG)


def draw_pair_list(key, part):
    group_count = N_IMG * N_REP
    slot_count = 2 * N_HEAD
    group_keys = jax.random.split(jax.random.fold_in(key, 11), group_count)
    orders = jax.vmap(permute_owners)(group_keys)
    owners = orders[:, jnp.arange(slot_count) % N_IMG]
    first_pick = jax.random.randint(jax.random.fold_in(key, 12), (group_count, slot_count), 0, IMG_DEV)
    second_pick = jax.random.randint(jax.random.fold_in(key, 13), (group_count, slot_count), 0, IMG_DEV)
    images = owners * IMG_DEV + jnp.minimum(first_pick, second_pick)
    images = images.reshape(N_IMG, N_REP, N_HEAD, 2).transpose(0, 2, 1, 3)
    return images.reshape(NPAIR, 2).astype(jnp.int32)


def block_levels(own_key, extent, cuts, smallest, largest):
    gain = 1.0
    for position, blocks in cuts:
        draws = jax.random.uniform(jax.random.fold_in(jax.random.fold_in(own_key, 6), position), (blocks,), jnp.float32, smallest / len(cuts), largest / len(cuts))
        gain = gain * jnp.repeat(jnp.exp(draws), extent[position] // blocks).reshape((-1,) + (1,) * (len(extent) - 1 - position))
    return gain


def bell_draw(key, extent, width, bound, shards=(), kind=jnp.bfloat16):
    drawn = width * jax.random.normal(key, extent, jnp.float32)
    if shards:
        drawn = drawn * block_levels(key, extent, shards, -0.22, 0.18)
    return jnp.clip(drawn, -bound, bound).astype(kind)


def setup_inputs(seed: int = 0, part: int = 0) -> dict:
    arg_keys = jax.random.split(jax.random.key(seed), 11)
    part_splits = jax.random.split(jax.random.fold_in(arg_keys[10], part), 11)
    return {
        "enc": bell_draw(part_splits[0], (NIMG, TOK, D_ENC), 1.0, 6.0, ((0, 4), (1, 2))),
        "pair_list": draw_pair_list(jax.random.fold_in(jax.random.fold_in(arg_keys[10], part), 71), part),
        "w_embed": bell_draw(arg_keys[2], (D_ENC, D), D_ENC ** -0.5, 0.1875, ((0, 2),)),
        "w_query": bell_draw(arg_keys[3], (D, D), (D // 3) ** -0.5, 0.375, ((0, 2),)),
        "w_key": bell_draw(arg_keys[4], (D, D), (D // 3) ** -0.5, 0.375, ((0, 2),)),
        "w_value": bell_draw(arg_keys[5], (D, D), D ** -0.5, 0.21875, ((0, 2),)),
        "w_out": bell_draw(arg_keys[6], (D, D), (D // 4) ** -0.5, 0.4375, ((0, 2),)),
        "w_head": bell_draw(arg_keys[7], (D, CHANNELS), D ** -0.5, 0.21875),
        "gain_query": jnp.clip(1.0 + 0.18 * jax.random.normal(arg_keys[8], (D,), jnp.float32), 0.1, 1.9),
        "gain_key": jnp.clip(1.0 + 0.18 * jax.random.normal(arg_keys[9], (D,), jnp.float32), 0.1, 1.9),
    }


NORM_EPSILON = 1e-06

def normalize(tensor, gain_vector):
    widened = tensor.astype(jnp.float32)
    center = widened - lax.optimization_barrier(jnp.mean(widened, axis=-1, keepdims=True))
    spread = lax.optimization_barrier(jnp.mean(center * center, axis=-1, keepdims=True))
    return center * lax.rsqrt(spread + NORM_EPSILON) * gain_vector

def matmul(left_side, right_side):
    return jnp.dot(left_side, right_side, preferred_element_type=jnp.float32)

def head_attention(operands):
    query_head, key_head, value_head = operands
    score_scale = query_head.shape[-1] ** (-0.5)
    scores = lax.dot_general(query_head, key_head, (((1,), (1,)), ((), ())), preferred_element_type=jnp.float32) * score_scale
    weights = jnp.exp(scores)
    probabilities = (weights / lax.optimization_barrier(jnp.sum(weights, axis=1, keepdims=True))).astype(jnp.bfloat16)
    return matmul(probabilities, value_head).astype(jnp.bfloat16)

def split_heads(tensor):
    token_count = tensor.shape[0]
    return tensor.reshape(token_count, HEADS, HEAD_DIM).transpose(1, 0, 2)

def decode_view(own_rows, key_rows, value_rows, gain_query, w_query, w_out, w_head):
    queries = matmul(normalize(own_rows, gain_query).astype(jnp.bfloat16), w_query).astype(jnp.bfloat16)
    attended = lax.map(head_attention, (split_heads(queries), split_heads(key_rows), split_heads(value_rows)))
    attended = attended.transpose(1, 0, 2).reshape(own_rows.shape[0], -1)
    residual = (own_rows.astype(jnp.float32) + matmul(attended, w_out)).astype(jnp.bfloat16)
    decoded = matmul(residual, w_head)
    confidence = 1.0 + jax.nn.softplus(decoded[:, -1:])
    weighted = jnp.concatenate([decoded[:, :-1] * confidence, confidence], axis=1)
    return weighted.T

def reference(enc, pair_list, w_embed, w_query, w_key, w_value, w_out, w_head, gain_query, gain_key):
    image_count = enc.shape[0]
    embedded = matmul(enc.reshape(-1, enc.shape[-1]), w_embed).astype(jnp.bfloat16)
    key_normed = normalize(embedded, gain_key).astype(jnp.bfloat16)
    key_rows = matmul(key_normed, w_key).astype(jnp.bfloat16).reshape(image_count, TOK, -1)
    value_rows = matmul(key_normed, w_value).astype(jnp.bfloat16).reshape(image_count, TOK, -1)
    embedded = embedded.reshape(image_count, TOK, -1)

    def one_pair(images):
        own_pair = embedded[images]
        key_pair = key_rows[images]
        value_pair = value_rows[images]
        toward = decode_view(own_pair[0], key_pair[1], value_pair[1], gain_query, w_query, w_out, w_head)
        backward = decode_view(own_pair[1], key_pair[0], value_pair[0], gain_query, w_query, w_out, w_head)
        return jnp.stack([toward, backward])
    contributions = lax.map(one_pair, pair_list.astype(jnp.int32))
    channel_count = contributions.shape[2]
    totals = jax.ops.segment_sum(contributions.reshape(-1, channel_count, TOK), pair_list.reshape(-1).astype(jnp.int32), num_segments=image_count)
    return totals[:, :-1] / jnp.maximum(totals[:, -1:], 1.0)
```

```python
import functools
import math

import jax
import jax.numpy as jnp
from jax import lax
from jax.experimental import pallas as pl
from jax.experimental.pallas import tpu as pltpu
from jax.sharding import PartitionSpec as P

HEAD_DIM = 64
NORM_EPSILON = 1e-06
LANES = 128
SPAN_PARTS = (3, 3, 2, 1)
VALUE_SCALE = 512.0
QUERY_SCALE = HEAD_DIM**-0.5 * math.log2(math.e)


def dot(left_side, right_side):
    return jnp.dot(left_side, right_side, preferred_element_type=jnp.float32)


def dot_nt(left_side, right_side):
    return lax.dot_general(
        left_side, right_side, (((1,), (1,)), ((), ())), preferred_element_type=jnp.float32
    )


def project_rows(rows, gq, gk, wq_ref, wk_ref, wv_ref):
    widened = rows.astype(jnp.float32)
    center = widened - jnp.mean(widened, axis=-1, keepdims=True)
    spread = jnp.mean(center * center, axis=-1, keepdims=True)
    base = center * lax.rsqrt(spread + NORM_EPSILON)
    query_in = (base * gq).astype(jnp.bfloat16)
    key_in = (base * gk).astype(jnp.bfloat16)
    queries = (dot(query_in, wq_ref[...]) * QUERY_SCALE).astype(jnp.bfloat16)
    keys = dot(key_in, wk_ref[...]).astype(jnp.bfloat16)
    values = (dot(key_in, wv_ref[...]) * (1.0 / VALUE_SCALE)).astype(jnp.bfloat16)
    return queries, keys, values


def decode_kernel(
    x_ref, wq_ref, wk_ref, wv_ref, wo_ref, wh_ref, gq_ref, gk_ref, out_ref, q_ref, k_ref, v_ref, att_ref
):
    tokens, width = x_ref.shape[1:]
    half = tokens // 2
    gq, gk = gq_ref[...], gk_ref[...]

    @pl.loop(0, 4)
    def _(step):
        side = step // 2
        rows = pl.ds(pl.multiple_of((step % 2) * half, half), half)
        queries, keys, values = project_rows(
            x_ref[side, rows, :], gq, gk, wq_ref, wk_ref, wv_ref
        )
        q_ref[side, rows, :] = queries
        k_ref[side, rows, :] = keys
        v_ref[side, rows, :] = values

    blocks = width // LANES

    @pl.loop(0, 2 * blocks)
    def _(step):
        side = step // blocks
        cols = pl.ds(pl.multiple_of(step % blocks * LANES, LANES), LANES)
        att_ref[side, :, cols] = attend_block(
            q_ref[side, :, cols], k_ref[1 - side, :, cols], v_ref[1 - side, :, cols]
        )

    @pl.loop(0, 2)
    def _(side):
        out_ref[side] = finish(x_ref[side], att_ref[side], wo_ref, wh_ref[...], out_ref.shape[1])


def decode(x, wq, wk, wv, wo, wht, gq, gk, channels):
    tokens, width = x.shape[1:]
    scratch = pltpu.VMEM((2, tokens, width), jnp.bfloat16)
    return pl.pallas_call(
        decode_kernel,
        out_shape=jax.ShapeDtypeStruct((2, channels, tokens), jnp.float32),
        scratch_shapes=[scratch] * 4,
        compiler_params=pltpu.CompilerParams(vmem_limit_bytes=48 * 2**20),
        name="decode",
    )(x, wq, wk, wv, wo, wht, gq, gk)


def attend_block(q, k, v):
    lane = lax.broadcasted_iota(jnp.int32, q.shape, 1)
    out = None
    for sub in range(LANES // HEAD_DIM):
        mine = (lane >= sub * HEAD_DIM) & (lane < (sub + 1) * HEAD_DIM)
        scores = dot_nt(jnp.where(mine, q, jnp.zeros_like(q)), k)
        weights = jnp.exp2(scores)
        inverse = 1.0 / jnp.sum(weights, axis=1, keepdims=True)
        probabilities = (weights * inverse).astype(jnp.bfloat16)
        part = dot(probabilities, v) * VALUE_SCALE
        out = part if out is None else jnp.where(mine, part, out)
    return out.astype(jnp.bfloat16)


def finish(own, attended, wo_ref, wh_rows, channels):
    residual = (own.astype(jnp.float32) + dot(attended, wo_ref[...])).astype(jnp.bfloat16)
    decoded = dot_nt(wh_rows, residual)
    last = decoded[channels - 1 : channels]
    confidence = 1.0 + jnp.maximum(last, 0.0) + jnp.log1p(jnp.exp(-jnp.abs(last)))
    row = lax.broadcasted_iota(jnp.int32, (channels, decoded.shape[1]), 0)
    return jnp.where(row == channels - 1, confidence, decoded[:channels] * confidence)


def fused_kernel(
    sizes, spans, pairs_hbm, enc_hbm, we_hbm, wq_hbm, wk_hbm, wv_hbm, wo_hbm, wh_ref, gq_ref, gk_ref, out_ref,
    enc_ref, we_ref, wq_ref, wk_ref, wv_ref, wo_ref, send_ref, land_refs, xs_refs, xr_refs,
    emb_ref, q_ref, k_ref, v_ref, att_ref, view_ref, part_ref, back_ref, pairs,
    pair_sem, enc_sem, wl_sem, ws_sem, wr_sem, zs_sem, zr_sem, xs_sem, xr_sem, bs_sem, br_sem,
):
    owners, heads, reps = sizes
    i, h, r = lax.axis_index("img"), lax.axis_index("head"), lax.axis_index("rep")
    images, rows = enc_ref.shape[:2]
    width = emb_ref.shape[2]
    blocks = width // LANES
    mesh_ids = pl.DeviceIdType.MESH
    count = owners * heads * reps
    me = (i * heads + h) * reps + r
    peer = (i * heads + (1 - h)) * reps + r

    pairs_copy = pltpu.make_async_copy(pairs_hbm, pairs, pair_sem)
    pairs_copy.start()
    weights = (
        (we_hbm, we_ref), (wk_hbm, wk_ref), (wv_hbm, wv_ref), (wq_hbm, wq_ref), (wo_hbm, wo_ref)
    )

    def place(n, rep):
        half, full = weights[n]
        depth = half.shape[0]
        return full.at[pl.ds(pl.multiple_of(rep * depth, depth), depth)]

    def weight_local(n):
        return pltpu.make_async_copy(weights[n][0], place(n, r), wl_sem.at[n])

    def weight_remote(n, step):
        return pltpu.make_async_remote_copy(
            src_ref=weights[n][0],
            dst_ref=place(n, r),
            send_sem=ws_sem.at[n, step],
            recv_sem=wr_sem.at[n, step],
            device_id={"rep": (r + step) % reps},
            device_id_type=mesh_ids,
        )

    weight_local(0).start()
    enc_copy = pltpu.make_async_copy(enc_hbm, enc_ref, enc_sem)
    enc_copy.start()
    for n in range(1, 5):
        weight_local(n).start()

    barrier = pltpu.get_barrier_semaphore()

    @pl.loop(1, count)
    def _(step):
        other = (me + step) % count
        pl.semaphore_signal(
            barrier,
            inc=1,
            device_id={
                "img": other // (heads * reps),
                "head": other // reps % heads,
                "rep": other % reps,
            },
            device_id_type=mesh_ids,
        )

    pl.semaphore_wait(barrier, count - 1)
    for n in range(5):
        for step in range(1, reps):
            weight_remote(n, step).start()

    def weight_wait(n):
        weight_local(n).wait()
        for step in range(1, reps):
            weight_remote(n, step).wait_recv()

    middle = owners // 2
    low = i // middle

    def source(k):
        base = (low + k // middle) % 2 * middle
        return base + (i % middle + k) % middle

    order = list(range(middle, owners)) + list(range(1, middle))

    def z_copy(d, c):
        offset, n = spans[c]
        return pltpu.make_async_remote_copy(
            src_ref=send_ref.at[d, pl.ds(offset, n)],
            dst_ref=land_refs[c].at[i],
            send_sem=zs_sem.at[d, c],
            recv_sem=zr_sem.at[i, c],
            device_id={"img": d},
            device_id_type=mesh_ids,
        )

    def z_arrival(a, c):
        offset, n = spans[c]
        return pltpu.make_async_remote_copy(
            src_ref=send_ref.at[a, pl.ds(offset, n)],
            dst_ref=land_refs[c].at[a],
            send_sem=zs_sem.at[a, c],
            recv_sem=zr_sem.at[a, c],
            device_id={"img": a},
            device_id_type=mesh_ids,
        )

    def x_copy(c):
        return pltpu.make_async_remote_copy(
            src_ref=xs_refs[c],
            dst_ref=xr_refs[c],
            send_sem=xs_sem.at[c],
            recv_sem=xr_sem.at[c],
            device_id={"head": 1 - h},
            device_id_type=mesh_ids,
        )

    pairs_copy.wait()
    enc_copy.wait()
    weight_wait(0)

    def pick_for(d):
        pick = 0
        for head in range(heads):
            for side in range(2):
                image = pairs[side, (d * heads + head) * reps + r]
                pick = pick + jnp.where(image // images == i, image % images, 0)
        return pick

    targets = [source(k) for k in order] + [i]
    picks = [pick_for(d) for d in targets]

    for c, (offset, n) in enumerate(spans):
        stacked = jnp.concatenate([enc_ref[pick, pl.ds(offset, n), :] for pick in picks], axis=0)
        embedded = dot(stacked, we_ref[...]).astype(jnp.bfloat16)
        for k, d in enumerate(targets):
            mine = embedded[k * n : (k + 1) * n]
            if k < owners - 1:
                send_ref[d, pl.ds(offset, n), :] = mine
                z_copy(d, c).start()
            else:
                land_refs[c][i] = mine

    lane = lax.broadcasted_iota(jnp.int32, (1, LANES), 1)
    first = lane < HEAD_DIM
    for offset, n in spans:
        for sub in range(2):
            ones = jnp.where(first == (sub == 0), 1.0, 0.0).astype(jnp.bfloat16)
            v_ref[:, :, pl.ds(4 * offset + 2 * n * sub, 2 * n), pl.ds(LANES, LANES)] = jnp.broadcast_to(
                ones[None, None], (2, blocks, 2 * n, LANES)
            )

    own = [pairs[side, me] // images for side in range(2)]
    other = [pairs[side, peer] // images for side in range(2)]
    for n in range(1, 4):
        weight_wait(n)
    gq, gk = gq_ref[...][None], gk_ref[...][None]
    zero = jnp.zeros((), jnp.bfloat16)

    def near_rows(c):
        offset, n = spans[c]
        return pl.ds(pl.multiple_of(h * rows + offset, 16), n)

    def far_rows(c):
        offset, n = spans[c]
        return pl.ds(pl.multiple_of((1 - h) * rows + offset, 16), n)

    def forward(c):
        for k in order:
            z_arrival(source(k), c).wait_recv()
        for side in range(2):
            xs_refs[c][side] = land_refs[c][other[side]]
        x_copy(c).start()

    def project(c):
        offset, n = spans[c]
        x_copy(c).wait_recv()
        parts = []
        for side in range(2):
            parts += [land_refs[c][own[side]], xr_refs[c][side]]
        for side in range(2):
            emb_ref[side, near_rows(c), :] = parts[2 * side]
            emb_ref[side, far_rows(c), :] = parts[2 * side + 1]
        queries, keys, values = project_rows(
            jnp.concatenate(parts, axis=0), gq, gk, wq_ref, wk_ref, wv_ref
        )
        for side in range(2):
            top = 2 * side * n
            q_ref[side, near_rows(c), :] = queries[top : top + n]
            q_ref[side, far_rows(c), :] = queries[top + n : top + 2 * n]
            for blk in range(blocks):
                cols = slice(blk * LANES, (blk + 1) * LANES)
                key, value = keys[top : top + 2 * n, cols], values[top : top + 2 * n, cols]
                for sub in range(2):
                    span = pl.ds(4 * offset + 2 * n * sub, 2 * n)
                    keep = first == (sub == 0)
                    k_ref[side, blk, span, :] = jnp.where(keep, key, zero)
                    v_ref[side, blk, span, pl.ds(0, LANES)] = jnp.where(keep, value, zero)

    last = len(spans) - 1
    forward(0)
    for c in range(1, last + 1):
        forward(c)
        project(c - 1)
    project(last)

    @pl.loop(0, 2 * blocks)
    def _(t):
        side, blk = t // blocks, t % blocks
        cols = pl.ds(pl.multiple_of(blk * LANES, LANES), LANES)
        for head in range(heads):
            span = pl.ds(head * rows, rows)
            scores = dot_nt(q_ref[side, span, cols], k_ref[1 - side, blk])
            powers = jnp.exp2(scores).astype(jnp.bfloat16)
            sums = dot(powers, v_ref[1 - side, blk])
            att_ref[side, span, cols] = (
                sums[:, :LANES] * (1.0 / sums[:, LANES:]) * VALUE_SCALE
            ).astype(jnp.bfloat16)

    weight_wait(4)
    shares = heads * reps
    channels = out_ref.shape[1] + 1
    part = out_ref.shape[2]
    wh_rows = wh_ref[...]
    for side in range(2):
        weighted = finish(emb_ref[side], att_ref[side], wo_ref, wh_rows, channels)
        for share in range(shares):
            view_ref[side, share] = weighted[:, share * part : (share + 1) * part].astype(
                view_ref.dtype
            )

    def b_copy(target):
        return pltpu.make_async_remote_copy(
            src_ref=part_ref.at[target],
            dst_ref=back_ref.at[me],
            send_sem=bs_sem.at[target],
            recv_sem=br_sem.at[me],
            device_id={
                "img": target // shares,
                "head": target // reps % heads,
                "rep": target % reps,
            },
            device_id_type=mesh_ids,
        )

    def b_arrival(src):
        return pltpu.make_async_remote_copy(
            src_ref=part_ref.at[src],
            dst_ref=back_ref.at[src],
            send_sem=bs_sem.at[src],
            recv_sem=br_sem.at[src],
            device_id={"img": src // shares, "head": src // reps % heads, "rep": src % reps},
            device_id_type=mesh_ids,
        )

    @pl.loop(0, count)
    def _(t):
        target = (1 - low) * (count - 1 - t) + low * t
        side = jnp.where(own[0] == target // shares, 0, 1)
        chosen = view_ref[side, target % shares]

        @pl.when(target == me)
        def _():
            back_ref[me] = chosen

        @pl.when(target != me)
        def _():
            part_ref[target] = chosen
            b_copy(target).start()

    @pl.loop(1, count)
    def _(step):
        b_arrival((me + step) % count).wait_recv()

    totals = [jnp.zeros(back_ref.shape[1:], jnp.float32) for _ in range(images)]
    for src in range(count):
        one, two = pairs[0, src], pairs[1, src]
        local = jnp.where(
            one // images == i,
            one % images,
            jnp.where(two // images == i, two % images, images),
        )
        block = back_ref[src].astype(jnp.float32)
        for image in range(images):
            totals[image] = totals[image] + jnp.where(local == image, block, 0.0)
    for image in range(images):
        total = totals[image]
        out_ref[image] = total[: channels - 1] / jnp.maximum(total[channels - 1 :], 1.0)

    for c in range(last + 1):
        for k in order:
            z_copy(source(k), c).wait_send()
        x_copy(c).wait_send()

    @pl.loop(1, count)
    def _(step):
        b_copy((me + step) % count).wait_send()

    for n in range(5):
        for step in range(1, reps):
            weight_remote(n, step).wait_send()


def fused(enc, pairs, w_embed, w_query, w_key, w_value, w_out, wht, gq, gk, spans):
    owners, heads, reps = (lax.axis_size(name) for name in ("img", "head", "rep"))
    images, rows, enc_width = enc.shape
    width = w_embed.shape[1]
    tokens = heads * rows
    part = rows // reps
    channels = wht.shape[0]
    count = owners * heads * reps
    blocks = width // LANES
    bf16 = jnp.bfloat16
    dma = pltpu.SemaphoreType.DMA
    full = pltpu.VMEM((width, width), bf16)
    any_space = pl.BlockSpec(memory_space=pl.ANY)
    vmem = pl.BlockSpec(memory_space=pltpu.VMEM)
    pieces = len(spans)
    return pl.pallas_call(
        functools.partial(fused_kernel, (owners, heads, reps), spans),
        out_shape=jax.ShapeDtypeStruct((images, channels - 1, part), jnp.float32),
        in_specs=[any_space] * 7 + [vmem] * 3,
        out_specs=vmem,
        scratch_shapes=[
            pltpu.VMEM(enc.shape, bf16),
            pltpu.VMEM((enc_width, width), bf16),
            full, full, full, full,
            pltpu.VMEM((owners, rows, width), bf16),
            tuple(pltpu.VMEM((owners, n, width), bf16) for _, n in spans),
            tuple(pltpu.VMEM((2, n, width), bf16) for _, n in spans),
            tuple(pltpu.VMEM((2, n, width), bf16) for _, n in spans),
            pltpu.VMEM((2, tokens, width), bf16),
            pltpu.VMEM((2, tokens, width), bf16),
            pltpu.VMEM((2, blocks, 2 * tokens, LANES), bf16),
            pltpu.VMEM((2, blocks, 2 * tokens, 2 * LANES), bf16),
            pltpu.VMEM((2, tokens, width), bf16),
            pltpu.VMEM((2, heads * reps, channels, part), bf16),
            pltpu.VMEM((count, channels, part), bf16),
            pltpu.VMEM((count, channels, part), bf16),
            pltpu.SMEM(pairs.shape, jnp.int32),
            dma(()),
            dma(()),
            dma((5,)),
            dma((5, reps)),
            dma((5, reps)),
            dma((owners, pieces)),
            dma((owners, pieces)),
            dma((pieces,)),
            dma((pieces,)),
            dma((count,)),
            dma((count,)),
        ],
        compiler_params=pltpu.CompilerParams(
            collective_id=0, has_side_effects=True, vmem_limit_bytes=56 * 2**20
        ),
        name="decode_views",
    )(pairs, enc, w_embed, w_query, w_key, w_value, w_out, wht, gq, gk)


def cut(rows):
    unit = rows // 9
    spans, offset = [], 0
    for parts in SPAN_PARTS:
        spans.append((offset, parts * unit))
        offset += parts * unit
    return tuple(spans)


def take_each(array, index):
    return jnp.stack(
        [lax.dynamic_index_in_dim(array, index[k], 0, keepdims=False) for k in range(index.shape[0])]
    )


def body(enc, pair_list, w_embed, w_query, w_key, w_value, w_out, w_head, gain_query, gain_key):
    owner_count = lax.axis_size("img")
    head_count = lax.axis_size("head")
    rep_count = lax.axis_size("rep")
    my_owner = lax.axis_index("img")
    my_rep = lax.axis_index("rep")
    img_count, row_count, enc_width = enc.shape
    slot_count = 2 * head_count
    assert slot_count == owner_count
    channels = w_head.shape[1]
    if head_count == 2 and rep_count == 2 and row_count % 144 == 0 and owner_count % 2 == 0:
        return fused(
            enc, pair_list.T, w_embed, w_query, w_key, w_value, w_out, w_head.T,
            gain_query, gain_key, cut(row_count),
        )
    wht = jnp.pad(w_head.T, ((0, -channels % 16), (0, 0)))
    full_embed, full_query, full_key, full_value, full_out = (
        lax.all_gather(w, "rep", axis=0, tiled=True)
        for w in (w_embed, w_query, w_key, w_value, w_out)
    )
    layout = lax.dynamic_index_in_dim(
        pair_list.reshape(owner_count, head_count, rep_count, 2), my_rep, 2, keepdims=False
    ).reshape(owner_count, slot_count)
    slot_owner = layout // img_count
    mine = slot_owner == my_owner
    pick = jnp.sum(jnp.where(mine, layout % img_count, 0), axis=1)
    group_owner = lax.dynamic_index_in_dim(slot_owner, my_owner, 0, keepdims=False)
    owner_index = group_owner.reshape(head_count, 2).T.reshape(-1)
    slot_of = jnp.sum(
        jnp.where(group_owner[None, :] == jnp.arange(slot_count)[:, None], jnp.arange(slot_count)[None, :], 0),
        axis=1,
    )

    rows = take_each(enc, pick).reshape(-1, enc_width)
    embedded = dot(rows, full_embed).astype(jnp.bfloat16).reshape(owner_count, row_count, -1)
    arrived = lax.all_to_all(embedded, "img", split_axis=0, concat_axis=0, tiled=True)
    grouped = take_each(arrived, owner_index).reshape(2, head_count, row_count, -1)
    spread = lax.all_to_all(grouped, "head", split_axis=1, concat_axis=1, tiled=True)
    x = spread.reshape(2, head_count * row_count, spread.shape[-1])
    weighted = decode(
        x, full_query, full_key, full_value, full_out, wht, gain_query[None], gain_key[None], channels
    )
    back = lax.all_to_all(
        weighted.reshape(2, channels, head_count, row_count),
        "head",
        split_axis=2,
        concat_axis=2,
        tiled=True,
    )
    by_slot = back.transpose(2, 0, 1, 3).reshape(slot_count, channels, row_count)
    received = lax.all_to_all(take_each(by_slot, slot_of), "img", split_axis=0, concat_axis=0, tiled=True)
    chosen = (pick[:, None] == jnp.arange(img_count)[None, :]).astype(jnp.float32)
    totals = jnp.einsum("qi,qxr->ixr", chosen, received, precision=lax.Precision.HIGHEST)
    shares = lax.psum_scatter(totals, "rep", scatter_dimension=2, tiled=True)
    return shares[:, :-1] / jnp.maximum(shares[:, -1:], 1.0)


def solution(mesh):
    in_specs = (
        P(("groups", "img"), "head", None),
        P("groups", None),
        P("rep", None),
        P("rep", None),
        P("rep", None),
        P("rep", None),
        P("rep", None),
        P(),
        P(),
        P(),
    )
    out_specs = P(("groups", "img"), None, ("head", "rep"))
    return jax.shard_map(body, mesh=mesh, in_specs=in_specs, out_specs=out_specs, check_vma=False)
```

```python
import functools
import math

import jax
import jax.numpy as jnp
from jax import lax
from jax.experimental import pallas as pl
from jax.experimental.pallas import tpu as pltpu
from jax.sharding import PartitionSpec as P

HEAD_DIM = 64
NORM_EPSILON = 1e-06
LANES = 128
SPAN_PARTS = (2, 2, 2, 2, 1)
GROUPS = (3, 4, 5)
AHEAD = 2
UNROLL = 4
VALUE_SCALE = 512.0
QUERY_SCALE = HEAD_DIM**-0.5 * math.log2(math.e)


def dot(left_side, right_side):
    return jnp.dot(left_side, right_side, preferred_element_type=jnp.float32)


def dot_nt(left_side, right_side):
    return lax.dot_general(
        left_side, right_side, (((1,), (1,)), ((), ())), preferred_element_type=jnp.float32
    )


def project_rows(rows, gq, gk, wq_ref, wk_ref, wv_ref):
    widened = rows.astype(jnp.float32)
    center = widened - jnp.mean(widened, axis=-1, keepdims=True)
    spread = jnp.mean(center * center, axis=-1, keepdims=True)
    base = center * lax.rsqrt(spread + NORM_EPSILON)
    query_in = (base * gq).astype(jnp.bfloat16)
    key_in = (base * gk).astype(jnp.bfloat16)
    queries = (dot(query_in, wq_ref[...]) * QUERY_SCALE).astype(jnp.bfloat16)
    keys = dot(key_in, wk_ref[...]).astype(jnp.bfloat16)
    values = (dot(key_in, wv_ref[...]) * (1.0 / VALUE_SCALE)).astype(jnp.bfloat16)
    return queries, keys, values


def decode_kernel(
    x_ref, wq_ref, wk_ref, wv_ref, wo_ref, wh_ref, gq_ref, gk_ref, out_ref, q_ref, k_ref, v_ref, att_ref
):
    tokens, width = x_ref.shape[1:]
    half = tokens // 2
    gq, gk = gq_ref[...], gk_ref[...]

    @pl.loop(0, 4)
    def _(step):
        side = step // 2
        rows = pl.ds(pl.multiple_of((step % 2) * half, half), half)
        queries, keys, values = project_rows(
            x_ref[side, rows, :], gq, gk, wq_ref, wk_ref, wv_ref
        )
        q_ref[side, rows, :] = queries
        k_ref[side, rows, :] = keys
        v_ref[side, rows, :] = values

    blocks = width // LANES

    @pl.loop(0, 2 * blocks)
    def _(step):
        side = step // blocks
        cols = pl.ds(pl.multiple_of(step % blocks * LANES, LANES), LANES)
        att_ref[side, :, cols] = attend_block(
            q_ref[side, :, cols], k_ref[1 - side, :, cols], v_ref[1 - side, :, cols]
        )

    @pl.loop(0, 2)
    def _(side):
        out_ref[side] = finish(x_ref[side], att_ref[side], wo_ref, wh_ref[...], out_ref.shape[1])


def decode(x, wq, wk, wv, wo, wht, gq, gk, channels):
    tokens, width = x.shape[1:]
    scratch = pltpu.VMEM((2, tokens, width), jnp.bfloat16)
    return pl.pallas_call(
        decode_kernel,
        out_shape=jax.ShapeDtypeStruct((2, channels, tokens), jnp.float32),
        scratch_shapes=[scratch] * 4,
        compiler_params=pltpu.CompilerParams(vmem_limit_bytes=48 * 2**20),
        name="decode",
    )(x, wq, wk, wv, wo, wht, gq, gk)


def attend_block(q, k, v):
    lane = lax.broadcasted_iota(jnp.int32, q.shape, 1)
    out = None
    for sub in range(LANES // HEAD_DIM):
        mine = (lane >= sub * HEAD_DIM) & (lane < (sub + 1) * HEAD_DIM)
        scores = dot_nt(jnp.where(mine, q, jnp.zeros_like(q)), k)
        weights = jnp.exp2(scores)
        inverse = 1.0 / jnp.sum(weights, axis=1, keepdims=True)
        probabilities = (weights * inverse).astype(jnp.bfloat16)
        part = dot(probabilities, v) * VALUE_SCALE
        out = part if out is None else jnp.where(mine, part, out)
    return out.astype(jnp.bfloat16)


def finish(own, attended, wo_ref, wh_rows, channels):
    residual = (own.astype(jnp.float32) + dot(attended, wo_ref[...])).astype(jnp.bfloat16)
    decoded = dot_nt(wh_rows, residual)
    last = decoded[channels - 1 : channels]
    confidence = 1.0 + jnp.maximum(last, 0.0) + jnp.log1p(jnp.exp(-jnp.abs(last)))
    row = lax.broadcasted_iota(jnp.int32, (channels, decoded.shape[1]), 0)
    return jnp.where(row == channels - 1, confidence, decoded[:channels] * confidence)


def fused_kernel(
    sizes, spans, pairs_hbm, enc_hbm, we_hbm, wq_hbm, wk_hbm, wv_hbm, wo_hbm, wh_ref, gq_ref, gk_ref, out_ref,
    enc_ref, we_ref, wq_ref, wk_ref, wv_ref, wo_ref, send_ref, land_refs, xs_refs, xr_refs,
    emb_ref, q_ref, k_ref, v_ref, att_ref, sum_ref, view_ref, part_ref, back_ref, pairs,
    pair_sem, enc_sem, wl_sem, ws_sem, wr_sem, zs_sem, zr_sem, xs_sem, xr_sem, bs_sem, br_sem,
):
    owners, heads, reps = sizes
    i, h, r = lax.axis_index("img"), lax.axis_index("head"), lax.axis_index("rep")
    images, rows = enc_ref.shape[:2]
    width = emb_ref.shape[2]
    blocks = width // LANES
    mesh_ids = pl.DeviceIdType.MESH
    count = owners * heads * reps
    me = (i * heads + h) * reps + r
    peer = (i * heads + (1 - h)) * reps + r

    pairs_copy = pltpu.make_async_copy(pairs_hbm, pairs, pair_sem)
    pairs_copy.start()
    weights = (
        (we_hbm, we_ref), (wk_hbm, wk_ref), (wv_hbm, wv_ref), (wq_hbm, wq_ref), (wo_hbm, wo_ref)
    )

    def place(n, rep):
        half, full = weights[n]
        depth = half.shape[0]
        return full.at[pl.ds(pl.multiple_of(rep * depth, depth), depth)]

    def weight_local(n):
        return pltpu.make_async_copy(weights[n][0], place(n, r), wl_sem.at[n])

    def weight_remote(n, step):
        return pltpu.make_async_remote_copy(
            src_ref=weights[n][0],
            dst_ref=place(n, r),
            send_sem=ws_sem.at[n, step],
            recv_sem=wr_sem.at[n, step],
            device_id={"rep": (r + step) % reps},
            device_id_type=mesh_ids,
        )

    weight_local(0).start()
    enc_copy = pltpu.make_async_copy(enc_hbm, enc_ref, enc_sem)
    enc_copy.start()
    for n in range(1, 5):
        weight_local(n).start()

    barrier = pltpu.get_barrier_semaphore()

    @pl.loop(1, count)
    def _(step):
        other = (me + step) % count
        pl.semaphore_signal(
            barrier,
            inc=1,
            device_id={
                "img": other // (heads * reps),
                "head": other // reps % heads,
                "rep": other % reps,
            },
            device_id_type=mesh_ids,
        )

    pl.semaphore_wait(barrier, count - 1)
    for step in range(1, reps):
        weight_remote(0, step).start()

    def weight_wait(n):
        weight_local(n).wait()
        for step in range(1, reps):
            weight_remote(n, step).wait_recv()

    middle = owners // 2
    low = i // middle

    def source(k):
        base = (low + k // middle) % 2 * middle
        return base + (i % middle + k) % middle

    order = list(range(middle, owners)) + list(range(1, middle))

    def z_copy(d, c):
        offset, n = spans[c]
        return pltpu.make_async_remote_copy(
            src_ref=send_ref.at[d, pl.ds(offset, n)],
            dst_ref=land_refs[c].at[i],
            send_sem=zs_sem.at[d, c],
            recv_sem=zr_sem.at[i, c],
            device_id={"img": d},
            device_id_type=mesh_ids,
        )

    def z_arrival(a, c):
        offset, n = spans[c]
        return pltpu.make_async_remote_copy(
            src_ref=send_ref.at[a, pl.ds(offset, n)],
            dst_ref=land_refs[c].at[a],
            send_sem=zs_sem.at[a, c],
            recv_sem=zr_sem.at[a, c],
            device_id={"img": a},
            device_id_type=mesh_ids,
        )

    def x_copy(c):
        return pltpu.make_async_remote_copy(
            src_ref=xs_refs[c],
            dst_ref=xr_refs[c],
            send_sem=xs_sem.at[c],
            recv_sem=xr_sem.at[c],
            device_id={"head": 1 - h},
            device_id_type=mesh_ids,
        )

    pairs_copy.wait()
    enc_copy.wait()
    weight_wait(0)

    def pick_for(d):
        pick = 0
        for head in range(heads):
            for side in range(2):
                image = pairs[side, (d * heads + head) * reps + r]
                pick = pick + jnp.where(image // images == i, image % images, 0)
        return pick

    targets = [source(k) for k in order] + [i]
    picks = [pick_for(d) for d in targets]

    for c, (offset, n) in enumerate(spans):
        stacked = jnp.concatenate([enc_ref[pick, pl.ds(offset, n), :] for pick in picks], axis=0)
        embedded = dot(stacked, we_ref[...]).astype(jnp.bfloat16)
        for k, d in enumerate(targets):
            mine = embedded[k * n : (k + 1) * n]
            if k < owners - 1:
                send_ref[d, pl.ds(offset, n), :] = mine
                if c < AHEAD:
                    z_copy(d, c).start()
            else:
                land_refs[c][i] = mine
        if c == 0:
            for w in range(1, 5):
                for step in range(1, reps):
                    weight_remote(w, step).start()

    lane = lax.broadcasted_iota(jnp.int32, (1, LANES), 1)
    first = lane < HEAD_DIM
    for offset, n in spans:
        for sub in range(2):
            ones = jnp.where(first == (sub == 0), 1.0, 0.0).astype(jnp.bfloat16)
            v_ref[:, :, pl.ds(4 * offset + 2 * n * sub, 2 * n), pl.ds(LANES, LANES)] = jnp.broadcast_to(
                ones[None, None], (2, blocks, 2 * n, LANES)
            )

    own = [pairs[side, me] // images for side in range(2)]
    other = [pairs[side, peer] // images for side in range(2)]
    for n in range(1, 4):
        weight_wait(n)
    gq, gk = gq_ref[...][None], gk_ref[...][None]
    zero = jnp.zeros((), jnp.bfloat16)

    def near_rows(c):
        offset, n = spans[c]
        return pl.ds(pl.multiple_of(h * rows + offset, 16), n)

    def far_rows(c):
        offset, n = spans[c]
        return pl.ds(pl.multiple_of((1 - h) * rows + offset, 16), n)

    def forward(c):
        for k in order:
            z_arrival(source(k), c).wait_recv()
        for side in range(2):
            xs_refs[c][side] = land_refs[c][other[side]]
        x_copy(c).start()

    def project(c):
        offset, n = spans[c]
        x_copy(c).wait_recv()
        parts = []
        for side in range(2):
            parts += [land_refs[c][own[side]], xr_refs[c][side]]
        for side in range(2):
            emb_ref[side, near_rows(c), :] = parts[2 * side]
            emb_ref[side, far_rows(c), :] = parts[2 * side + 1]
        queries, keys, values = project_rows(
            jnp.concatenate(parts, axis=0), gq, gk, wq_ref, wk_ref, wv_ref
        )
        for side in range(2):
            top = 2 * side * n
            q_ref[side, near_rows(c), :] = queries[top : top + n]
            q_ref[side, far_rows(c), :] = queries[top + n : top + 2 * n]
            for blk in range(blocks):
                cols = slice(blk * LANES, (blk + 1) * LANES)
                key, value = keys[top : top + 2 * n, cols], values[top : top + 2 * n, cols]
                for sub in range(2):
                    span = pl.ds(4 * offset + 2 * n * sub, 2 * n)
                    keep = first == (sub == 0)
                    k_ref[side, blk, span, :] = jnp.where(keep, key, zero)
                    v_ref[side, blk, span, pl.ds(0, LANES)] = jnp.where(keep, value, zero)

    def attend(steps):
        @pl.loop(0, 2 * blocks // UNROLL)
        def _(t):
            items = []
            for u in range(UNROLL):
                place = t * UNROLL + u
                for step in steps:
                    items.append((place // blocks, place % blocks, step))

            def lanes(blk):
                return pl.ds(pl.multiple_of(blk * LANES, LANES), LANES)

            def score(item):
                side, blk, (pieces, keys, _, _) = item
                queries = [q_ref[side, pl.ds(start, n), lanes(blk)] for start, n in pieces]
                joined = queries[0] if len(queries) == 1 else jnp.concatenate(queries, axis=0)
                return dot_nt(joined, k_ref[1 - side, blk, keys])

            scores = score(items[0])
            for place, item in enumerate(items):
                later = score(items[place + 1]) if place + 1 < len(items) else None
                side, blk, (pieces, keys, adds, ends) = item
                sums = dot(jnp.exp2(scores).astype(jnp.bfloat16), v_ref[1 - side, blk, keys])
                top = 0
                for start, n in pieces:
                    rows_here = pl.ds(start, n)
                    mine = sums[top : top + n]
                    top += n
                    if adds:
                        mine = mine + sum_ref[side, blk, rows_here]
                    if ends:
                        att_ref[side, rows_here, lanes(blk)] = (
                            mine[:, :LANES] * (1.0 / mine[:, LANES:]) * VALUE_SCALE
                        ).astype(jnp.bfloat16)
                    else:
                        sum_ref[side, blk, rows_here] = mine
                scores = later

    def old_steps(g):
        low_row, high_row = edges[g], edges[g + 1]
        ends = g == len(GROUPS) - 1
        return [
            (((head * rows, low_row),), pl.ds(4 * low_row, 4 * (high_row - low_row)), True, ends)
            for head in range(heads)
        ]

    def new_steps(g):
        low_row, high_row = edges[g], edges[g + 1]
        ends = g == len(GROUPS) - 1
        pieces = tuple((head * rows + low_row, high_row - low_row) for head in range(heads))
        if high_row - low_row > 128:
            return [((piece,), pl.ds(0, 4 * high_row), False, ends) for piece in pieces]
        return [(pieces, pl.ds(0, 4 * high_row), False, ends)]

    last = len(spans) - 1
    edges = [0] + [sum(spans[g - 1]) for g in GROUPS]
    done = 0
    for c in range(last + 1):
        forward(c)
        if c + AHEAD <= last:
            for k in order:
                z_copy(source(k), c + AHEAD).start()
        if c > 0:
            project(c - 1)
            if c in GROUPS:
                g = GROUPS.index(c)
                attend((old_steps(g) if g else []) + new_steps(g))
    project(last)
    attend(old_steps(len(GROUPS) - 1) + new_steps(len(GROUPS) - 1))

    weight_wait(4)
    shares = heads * reps
    channels = out_ref.shape[0] + 1
    part = out_ref.shape[2]
    wh_rows = wh_ref[...]
    for side in range(2):
        weighted = finish(emb_ref[side], att_ref[side], wo_ref, wh_rows, channels)
        for share in range(shares):
            view_ref[side, share] = weighted[:, share * part : (share + 1) * part].astype(
                view_ref.dtype
            )

    def b_copy(target):
        return pltpu.make_async_remote_copy(
            src_ref=part_ref.at[target],
            dst_ref=back_ref.at[me],
            send_sem=bs_sem.at[target],
            recv_sem=br_sem.at[me],
            device_id={
                "img": target // shares,
                "head": target // reps % heads,
                "rep": target % reps,
            },
            device_id_type=mesh_ids,
        )

    def b_arrival(src):
        return pltpu.make_async_remote_copy(
            src_ref=part_ref.at[src],
            dst_ref=back_ref.at[src],
            send_sem=bs_sem.at[src],
            recv_sem=br_sem.at[src],
            device_id={"img": src // shares, "head": src // reps % heads, "rep": src % reps},
            device_id_type=mesh_ids,
        )

    @pl.loop(0, count)
    def _(t):
        target = (1 - low) * (count - 1 - t) + low * t
        side = jnp.where(own[0] == target // shares, 0, 1)
        chosen = view_ref[side, target % shares]

        @pl.when(target == me)
        def _():
            back_ref[me] = chosen

        @pl.when(target != me)
        def _():
            part_ref[target] = chosen
            b_copy(target).start()

    @pl.loop(1, count)
    def _(step):
        b_arrival((me + step) % count).wait_recv()

    totals = [jnp.zeros(back_ref.shape[1:], jnp.float32) for _ in range(images)]
    for src in range(count):
        one, two = pairs[0, src], pairs[1, src]
        local = jnp.where(
            one // images == i,
            one % images,
            jnp.where(two // images == i, two % images, images),
        )
        block = back_ref[src].astype(jnp.float32)
        for image in range(images):
            totals[image] = totals[image] + jnp.where(local == image, block, 0.0)
    for image in range(images):
        total = totals[image]
        out_ref[:, image, :] = total[: channels - 1] / jnp.maximum(total[channels - 1 :], 1.0)

    for c in range(last + 1):
        for k in order:
            z_copy(source(k), c).wait_send()
        x_copy(c).wait_send()

    @pl.loop(1, count)
    def _(step):
        b_copy((me + step) % count).wait_send()

    for n in range(5):
        for step in range(1, reps):
            weight_remote(n, step).wait_send()


def fused(enc, pairs, w_embed, w_query, w_key, w_value, w_out, wht, gq, gk, spans):
    owners, heads, reps = (lax.axis_size(name) for name in ("img", "head", "rep"))
    images, rows, enc_width = enc.shape
    width = w_embed.shape[1]
    tokens = heads * rows
    part = rows // reps
    channels = wht.shape[0]
    count = owners * heads * reps
    blocks = width // LANES
    bf16 = jnp.bfloat16
    dma = pltpu.SemaphoreType.DMA
    full = pltpu.VMEM((width, width), bf16)
    any_space = pl.BlockSpec(memory_space=pl.ANY)
    vmem = pl.BlockSpec(memory_space=pltpu.VMEM)
    pieces = len(spans)
    return pl.pallas_call(
        functools.partial(fused_kernel, (owners, heads, reps), spans),
        out_shape=jax.ShapeDtypeStruct((channels - 1, images, part), jnp.float32),
        in_specs=[any_space] * 7 + [vmem] * 3,
        out_specs=vmem,
        scratch_shapes=[
            pltpu.VMEM(enc.shape, bf16),
            pltpu.VMEM((enc_width, width), bf16),
            full, full, full, full,
            pltpu.VMEM((owners, rows, width), bf16),
            tuple(pltpu.VMEM((owners, n, width), bf16) for _, n in spans),
            tuple(pltpu.VMEM((2, n, width), bf16) for _, n in spans),
            tuple(pltpu.VMEM((2, n, width), bf16) for _, n in spans),
            pltpu.VMEM((2, tokens, width), bf16),
            pltpu.VMEM((2, tokens, width), bf16),
            pltpu.VMEM((2, blocks, 2 * tokens, LANES), bf16),
            pltpu.VMEM((2, blocks, 2 * tokens, 2 * LANES), bf16),
            pltpu.VMEM((2, tokens, width), bf16),
            pltpu.VMEM((2, blocks, tokens, 2 * LANES), jnp.float32),
            pltpu.VMEM((2, heads * reps, channels, part), bf16),
            pltpu.VMEM((count, channels, part), bf16),
            pltpu.VMEM((count, channels, part), bf16),
            pltpu.SMEM(pairs.shape, jnp.int32),
            dma(()),
            dma(()),
            dma((5,)),
            dma((5, reps)),
            dma((5, reps)),
            dma((owners, pieces)),
            dma((owners, pieces)),
            dma((pieces,)),
            dma((pieces,)),
            dma((count,)),
            dma((count,)),
        ],
        compiler_params=pltpu.CompilerParams(
            collective_id=0, has_side_effects=True, vmem_limit_bytes=56 * 2**20
        ),
        name="decode_views",
    )(pairs, enc, w_embed, w_query, w_key, w_value, w_out, wht, gq, gk).transpose(1, 0, 2)


def cut(rows):
    unit = rows // 9
    spans, offset = [], 0
    for parts in SPAN_PARTS:
        spans.append((offset, parts * unit))
        offset += parts * unit
    return tuple(spans)


def take_each(array, index):
    return jnp.stack(
        [lax.dynamic_index_in_dim(array, index[k], 0, keepdims=False) for k in range(index.shape[0])]
    )


def body(enc, pair_list, w_embed, w_query, w_key, w_value, w_out, w_head, gain_query, gain_key):
    owner_count = lax.axis_size("img")
    head_count = lax.axis_size("head")
    rep_count = lax.axis_size("rep")
    my_owner = lax.axis_index("img")
    my_rep = lax.axis_index("rep")
    img_count, row_count, enc_width = enc.shape
    slot_count = 2 * head_count
    assert slot_count == owner_count
    channels = w_head.shape[1]
    if head_count == 2 and rep_count == 2 and row_count % 144 == 0 and owner_count % 2 == 0:
        return fused(
            enc, pair_list.T, w_embed, w_query, w_key, w_value, w_out, w_head.T,
            gain_query, gain_key, cut(row_count),
        )
    wht = jnp.pad(w_head.T, ((0, -channels % 16), (0, 0)))
    full_embed, full_query, full_key, full_value, full_out = (
        lax.all_gather(w, "rep", axis=0, tiled=True)
        for w in (w_embed, w_query, w_key, w_value, w_out)
    )
    layout = lax.dynamic_index_in_dim(
        pair_list.reshape(owner_count, head_count, rep_count, 2), my_rep, 2, keepdims=False
    ).reshape(owner_count, slot_count)
    slot_owner = layout // img_count
    mine = slot_owner == my_owner
    pick = jnp.sum(jnp.where(mine, layout % img_count, 0), axis=1)
    group_owner = lax.dynamic_index_in_dim(slot_owner, my_owner, 0, keepdims=False)
    owner_index = group_owner.reshape(head_count, 2).T.reshape(-1)
    slot_of = jnp.sum(
        jnp.where(group_owner[None, :] == jnp.arange(slot_count)[:, None], jnp.arange(slot_count)[None, :], 0),
        axis=1,
    )

    rows = take_each(enc, pick).reshape(-1, enc_width)
    embedded = dot(rows, full_embed).astype(jnp.bfloat16).reshape(owner_count, row_count, -1)
    arrived = lax.all_to_all(embedded, "img", split_axis=0, concat_axis=0, tiled=True)
    grouped = take_each(arrived, owner_index).reshape(2, head_count, row_count, -1)
    spread = lax.all_to_all(grouped, "head", split_axis=1, concat_axis=1, tiled=True)
    x = spread.reshape(2, head_count * row_count, spread.shape[-1])
    weighted = decode(
        x, full_query, full_key, full_value, full_out, wht, gain_query[None], gain_key[None], channels
    )
    back = lax.all_to_all(
        weighted.reshape(2, channels, head_count, row_count),
        "head",
        split_axis=2,
        concat_axis=2,
        tiled=True,
    )
    by_slot = back.transpose(2, 0, 1, 3).reshape(slot_count, channels, row_count)
    received = lax.all_to_all(take_each(by_slot, slot_of), "img", split_axis=0, concat_axis=0, tiled=True)
    chosen = (pick[:, None] == jnp.arange(img_count)[None, :]).astype(jnp.float32)
    totals = jnp.einsum("qi,qxr->ixr", chosen, received, precision=lax.Precision.HIGHEST)
    shares = lax.psum_scatter(totals, "rep", scatter_dimension=2, tiled=True)
    return shares[:, :-1] / jnp.maximum(shares[:, -1:], 1.0)


def solution(mesh):
    in_specs = (
        P(("groups", "img"), "head", None),
        P("groups", None),
        P("rep", None),
        P("rep", None),
        P("rep", None),
        P("rep", None),
        P("rep", None),
        P(),
        P(),
        P(),
    )
    out_specs = P(("groups", "img"), None, ("head", "rep"))
    return jax.shard_map(body, mesh=mesh, in_specs=in_specs, out_specs=out_specs, check_vma=False)
```

```python
import functools
import math

import jax
import jax.numpy as jnp
from jax import lax
from jax.experimental import pallas as pl
from jax.experimental.pallas import tpu as pltpu
from jax.sharding import PartitionSpec as P

HEAD_DIM = 64
NORM_EPSILON = 1e-06
LANES = 128
SPAN_PARTS = (1,) * 9
GROUPS = (4, 7, 9)
QUOTA = 2
AHEAD = 2
UNROLL = 4
VALUE_SCALE = 512.0
QUERY_SCALE = HEAD_DIM**-0.5 * math.log2(math.e)


def dot(left_side, right_side):
    return jnp.dot(left_side, right_side, preferred_element_type=jnp.float32)


def dot_nt(left_side, right_side):
    return lax.dot_general(
        left_side, right_side, (((1,), (1,)), ((), ())), preferred_element_type=jnp.float32
    )


def project_rows(rows, gq, gk, wq_ref, wk_ref, wv_ref):
    widened = rows.astype(jnp.float32)
    center = widened - jnp.mean(widened, axis=-1, keepdims=True)
    spread = jnp.mean(center * center, axis=-1, keepdims=True)
    base = center * lax.rsqrt(spread + NORM_EPSILON)
    query_in = (base * gq).astype(jnp.bfloat16)
    key_in = (base * gk).astype(jnp.bfloat16)
    queries = (dot(query_in, wq_ref[...]) * QUERY_SCALE).astype(jnp.bfloat16)
    keys = dot(key_in, wk_ref[...]).astype(jnp.bfloat16)
    values = (dot(key_in, wv_ref[...]) * (1.0 / VALUE_SCALE)).astype(jnp.bfloat16)
    return queries, keys, values


def decode_kernel(
    x_ref, wq_ref, wk_ref, wv_ref, wo_ref, wh_ref, gq_ref, gk_ref, out_ref, q_ref, k_ref, v_ref, att_ref
):
    tokens, width = x_ref.shape[1:]
    half = tokens // 2
    gq, gk = gq_ref[...], gk_ref[...]

    @pl.loop(0, 4)
    def _(step):
        side = step // 2
        rows = pl.ds(pl.multiple_of((step % 2) * half, half), half)
        queries, keys, values = project_rows(
            x_ref[side, rows, :], gq, gk, wq_ref, wk_ref, wv_ref
        )
        q_ref[side, rows, :] = queries
        k_ref[side, rows, :] = keys
        v_ref[side, rows, :] = values

    blocks = width // LANES

    @pl.loop(0, 2 * blocks)
    def _(step):
        side = step // blocks
        cols = pl.ds(pl.multiple_of(step % blocks * LANES, LANES), LANES)
        att_ref[side, :, cols] = attend_block(
            q_ref[side, :, cols], k_ref[1 - side, :, cols], v_ref[1 - side, :, cols]
        )

    @pl.loop(0, 2)
    def _(side):
        out_ref[side] = finish(x_ref[side], att_ref[side], wo_ref, wh_ref[...], out_ref.shape[1])


def decode(x, wq, wk, wv, wo, wht, gq, gk, channels):
    tokens, width = x.shape[1:]
    scratch = pltpu.VMEM((2, tokens, width), jnp.bfloat16)
    return pl.pallas_call(
        decode_kernel,
        out_shape=jax.ShapeDtypeStruct((2, channels, tokens), jnp.float32),
        scratch_shapes=[scratch] * 4,
        compiler_params=pltpu.CompilerParams(vmem_limit_bytes=48 * 2**20),
        name="decode",
    )(x, wq, wk, wv, wo, wht, gq, gk)


def attend_block(q, k, v):
    lane = lax.broadcasted_iota(jnp.int32, q.shape, 1)
    out = None
    for sub in range(LANES // HEAD_DIM):
        mine = (lane >= sub * HEAD_DIM) & (lane < (sub + 1) * HEAD_DIM)
        scores = dot_nt(jnp.where(mine, q, jnp.zeros_like(q)), k)
        weights = jnp.exp2(scores)
        inverse = 1.0 / jnp.sum(weights, axis=1, keepdims=True)
        probabilities = (weights * inverse).astype(jnp.bfloat16)
        part = dot(probabilities, v) * VALUE_SCALE
        out = part if out is None else jnp.where(mine, part, out)
    return out.astype(jnp.bfloat16)


def finish(own, attended, wo_ref, wh_rows, channels):
    residual = (own.astype(jnp.float32) + dot(attended, wo_ref[...])).astype(jnp.bfloat16)
    decoded = dot_nt(wh_rows, residual)
    last = decoded[channels - 1 : channels]
    confidence = 1.0 + jnp.maximum(last, 0.0) + jnp.log1p(jnp.exp(-jnp.abs(last)))
    row = lax.broadcasted_iota(jnp.int32, (channels, decoded.shape[1]), 0)
    return jnp.where(row == channels - 1, confidence, decoded[:channels] * confidence)


def fused_kernel(
    sizes, spans, pairs_hbm, enc_hbm, we_hbm, wq_hbm, wk_hbm, wv_hbm, wo_hbm, wh_ref, gq_ref, gk_ref, out_ref,
    enc_ref, we_ref, wq_ref, wk_ref, wv_ref, wo_ref, send_ref, land_refs, xs_refs, xr_refs,
    emb_ref, q_ref, k_ref, v_ref, att_ref, sum_ref, view_ref, part_ref, back_ref, pairs,
    pair_sem, enc_sem, wl_sem, ws_sem, wr_sem, zs_sem, zr_sem, xs_sem, xr_sem, bs_sem, br_sem,
):
    owners, heads, reps = sizes
    i, h, r = lax.axis_index("img"), lax.axis_index("head"), lax.axis_index("rep")
    images, rows = enc_ref.shape[:2]
    width = emb_ref.shape[2]
    blocks = width // LANES
    mesh_ids = pl.DeviceIdType.MESH
    count = owners * heads * reps
    me = (i * heads + h) * reps + r
    peer = (i * heads + (1 - h)) * reps + r

    pairs_copy = pltpu.make_async_copy(pairs_hbm, pairs, pair_sem)
    pairs_copy.start()
    weights = (
        (we_hbm, we_ref), (wk_hbm, wk_ref), (wv_hbm, wv_ref), (wq_hbm, wq_ref), (wo_hbm, wo_ref)
    )

    def place(n, rep):
        half, full = weights[n]
        depth = half.shape[0]
        return full.at[pl.ds(pl.multiple_of(rep * depth, depth), depth)]

    def weight_local(n):
        return pltpu.make_async_copy(weights[n][0], place(n, r), wl_sem.at[n])

    def weight_remote(n, step):
        return pltpu.make_async_remote_copy(
            src_ref=weights[n][0],
            dst_ref=place(n, r),
            send_sem=ws_sem.at[n, step],
            recv_sem=wr_sem.at[n, step],
            device_id={"rep": (r + step) % reps},
            device_id_type=mesh_ids,
        )

    weight_local(0).start()
    enc_copy = pltpu.make_async_copy(enc_hbm, enc_ref, enc_sem)
    enc_copy.start()
    for n in range(1, 5):
        weight_local(n).start()

    barrier = pltpu.get_barrier_semaphore()

    neighbours = [{"img": (i + step) % owners} for step in range(1, owners)]
    neighbours += [{"head": 1 - h}, {"rep": 1 - r}]
    for neighbour in neighbours:
        pl.semaphore_signal(barrier, inc=1, device_id=neighbour, device_id_type=mesh_ids)
    pl.semaphore_wait(barrier, len(neighbours))
    for step in range(1, reps):
        weight_remote(0, step).start()

    def weight_wait(n):
        weight_local(n).wait()
        for step in range(1, reps):
            weight_remote(n, step).wait_recv()

    middle = owners // 2
    low = i // middle

    def source(k):
        base = (low + k // middle) % 2 * middle
        return base + (i % middle + k) % middle

    order = list(range(middle, owners)) + list(range(1, middle))

    def z_copy(d, c):
        offset, n = spans[c]
        return pltpu.make_async_remote_copy(
            src_ref=send_ref.at[d, pl.ds(offset, n)],
            dst_ref=land_refs[c].at[i],
            send_sem=zs_sem.at[d, c],
            recv_sem=zr_sem.at[i, c],
            device_id={"img": d},
            device_id_type=mesh_ids,
        )

    def z_arrival(a, c):
        offset, n = spans[c]
        return pltpu.make_async_remote_copy(
            src_ref=send_ref.at[a, pl.ds(offset, n)],
            dst_ref=land_refs[c].at[a],
            send_sem=zs_sem.at[a, c],
            recv_sem=zr_sem.at[a, c],
            device_id={"img": a},
            device_id_type=mesh_ids,
        )

    def x_copy(c):
        return pltpu.make_async_remote_copy(
            src_ref=xs_refs[c],
            dst_ref=xr_refs[c],
            send_sem=xs_sem.at[c],
            recv_sem=xr_sem.at[c],
            device_id={"head": 1 - h},
            device_id_type=mesh_ids,
        )

    pairs_copy.wait()
    enc_copy.wait()
    weight_wait(0)

    def pick_for(d):
        pick = 0
        for head in range(heads):
            for side in range(2):
                image = pairs[side, (d * heads + head) * reps + r]
                pick = pick + jnp.where(image // images == i, image % images, 0)
        return pick

    targets = [source(k) for k in order] + [i]
    picks = [pick_for(d) for d in targets]

    for c, (offset, n) in enumerate(spans):
        stacked = jnp.concatenate([enc_ref[pick, pl.ds(offset, n), :] for pick in picks], axis=0)
        embedded = dot(stacked, we_ref[...]).astype(jnp.bfloat16)
        for k, d in enumerate(targets):
            mine = embedded[k * n : (k + 1) * n]
            if k < owners - 1:
                send_ref[d, pl.ds(offset, n), :] = mine
                if c < AHEAD:
                    z_copy(d, c).start()
            else:
                land_refs[c][i] = mine
        if c == 0:
            for w in range(1, 5):
                for step in range(1, reps):
                    weight_remote(w, step).start()

    lane = lax.broadcasted_iota(jnp.int32, (1, LANES), 1)
    first = lane < HEAD_DIM
    for offset, n in spans:
        for sub in range(2):
            ones = jnp.where(first == (sub == 0), 1.0, 0.0).astype(jnp.bfloat16)
            v_ref[:, :, pl.ds(4 * offset + 2 * n * sub, 2 * n), pl.ds(LANES, LANES)] = jnp.broadcast_to(
                ones[None, None], (2, blocks, 2 * n, LANES)
            )

    own = [pairs[side, me] // images for side in range(2)]
    other = [pairs[side, peer] // images for side in range(2)]
    for n in range(1, 4):
        weight_wait(n)
    gq, gk = gq_ref[...][None], gk_ref[...][None]
    zero = jnp.zeros((), jnp.bfloat16)

    def near_rows(c):
        offset, n = spans[c]
        return pl.ds(pl.multiple_of(h * rows + offset, 16), n)

    def far_rows(c):
        offset, n = spans[c]
        return pl.ds(pl.multiple_of((1 - h) * rows + offset, 16), n)

    def forward(c):
        for k in order:
            z_arrival(source(k), c).wait_recv()
        for side in range(2):
            xs_refs[c][side] = land_refs[c][other[side]]
        x_copy(c).start()

    def project(c):
        offset, n = spans[c]
        x_copy(c).wait_recv()
        parts = []
        for side in range(2):
            parts += [land_refs[c][own[side]], xr_refs[c][side]]
        for side in range(2):
            emb_ref[side, near_rows(c), :] = parts[2 * side]
            emb_ref[side, far_rows(c), :] = parts[2 * side + 1]
        queries, keys, values = project_rows(
            jnp.concatenate(parts, axis=0), gq, gk, wq_ref, wk_ref, wv_ref
        )
        for side in range(2):
            top = 2 * side * n
            q_ref[side, near_rows(c), :] = queries[top : top + n]
            q_ref[side, far_rows(c), :] = queries[top + n : top + 2 * n]
            for blk in range(blocks):
                cols = slice(blk * LANES, (blk + 1) * LANES)
                key, value = keys[top : top + 2 * n, cols], values[top : top + 2 * n, cols]
                for sub in range(2):
                    span = pl.ds(4 * offset + 2 * n * sub, 2 * n)
                    keep = first == (sub == 0)
                    k_ref[side, blk, span, :] = jnp.where(keep, key, zero)
                    v_ref[side, blk, span, pl.ds(0, LANES)] = jnp.where(keep, value, zero)

    def attend(steps, begin, end):
        @pl.loop(begin, end)
        def _(t):
            items = []
            for u in range(UNROLL):
                place = t * UNROLL + u
                for step in steps:
                    items.append((place // blocks, place % blocks, step))

            def lanes(blk):
                return pl.ds(pl.multiple_of(blk * LANES, LANES), LANES)

            def score(item):
                side, blk, (pieces, keys, _, _) = item
                queries = [q_ref[side, pl.ds(start, n), lanes(blk)] for start, n in pieces]
                joined = queries[0] if len(queries) == 1 else jnp.concatenate(queries, axis=0)
                return dot_nt(joined, k_ref[1 - side, blk, keys])

            scores = score(items[0])
            for place, item in enumerate(items):
                later = score(items[place + 1]) if place + 1 < len(items) else None
                side, blk, (pieces, keys, adds, ends) = item
                sums = dot(jnp.exp2(scores).astype(jnp.bfloat16), v_ref[1 - side, blk, keys])
                top = 0
                for start, n in pieces:
                    rows_here = pl.ds(start, n)
                    mine = sums[top : top + n]
                    top += n
                    if adds:
                        mine = mine + sum_ref[side, blk, rows_here]
                    if ends:
                        att_ref[side, rows_here, lanes(blk)] = (
                            mine[:, :LANES] * (1.0 / mine[:, LANES:]) * VALUE_SCALE
                        ).astype(jnp.bfloat16)
                    else:
                        sum_ref[side, blk, rows_here] = mine
                scores = later

    def old_steps(g):
        low_row, high_row = edges[g], edges[g + 1]
        ends = g == len(GROUPS) - 1
        return [
            (((head * rows, low_row),), pl.ds(4 * low_row, 4 * (high_row - low_row)), True, ends)
            for head in range(heads)
        ]

    def new_steps(g):
        low_row, high_row = edges[g], edges[g + 1]
        ends = g == len(GROUPS) - 1
        pieces = tuple((head * rows + low_row, high_row - low_row) for head in range(heads))
        if high_row - low_row > 128:
            return [((piece,), pl.ds(0, 4 * high_row), False, ends) for piece in pieces]
        return [(pieces, pl.ds(0, 4 * high_row), False, ends)]

    last = len(spans) - 1
    edges = [0] + [sum(spans[g - 1]) for g in GROUPS]
    turns = 2 * blocks // UNROLL
    ready = []
    for c in range(last + 1):
        forward(c)
        if c + AHEAD <= last:
            for k in order:
                z_copy(source(k), c + AHEAD).start()
        if c > 0:
            project(c - 1)
        if c in GROUPS:
            g = GROUPS.index(c)
            ready += [((old_steps(g) if g else []) + new_steps(g), turn) for turn in range(turns)]
        for steps, turn in ready[:QUOTA]:
            attend(steps, turn, turn + 1)
        ready = ready[QUOTA:]
    for steps, turn in ready:
        attend(steps, turn, turn + 1)
    project(last)
    attend(old_steps(len(GROUPS) - 1) + new_steps(len(GROUPS) - 1), 0, turns)

    weight_wait(4)
    shares = heads * reps
    channels = out_ref.shape[0] + 1
    part = out_ref.shape[2]
    wh_rows = wh_ref[...]
    extra = part - LANES
    strips = channels // 4
    order_rows = [(share * part, LANES) for share in range(shares)]
    order_rows += [(share * part + LANES, extra) for share in range(shares)]

    def arrange(ref, side):
        return jnp.concatenate([ref[side, pl.ds(start, n), :] for start, n in order_rows], axis=0)

    for side in range(2):
        weighted = finish(arrange(emb_ref, side), arrange(att_ref, side), wo_ref, wh_rows, channels)
        for share in range(shares):
            left = shares * LANES + share * extra
            strip = [weighted[4 * g : 4 * g + 4, left : left + extra] for g in range(strips)]
            strip.append(jnp.zeros((4, LANES - strips * extra), jnp.float32))
            packed = jnp.concatenate(
                [weighted[:, share * LANES : (share + 1) * LANES], jnp.concatenate(strip, axis=1)], axis=0
            )
            view_ref[side, share] = packed.astype(view_ref.dtype)

    def b_copy(target):
        return pltpu.make_async_remote_copy(
            src_ref=part_ref.at[target],
            dst_ref=back_ref.at[me],
            send_sem=bs_sem.at[target],
            recv_sem=br_sem.at[me],
            device_id={
                "img": target // shares,
                "head": target // reps % heads,
                "rep": target % reps,
            },
            device_id_type=mesh_ids,
        )

    def b_arrival(src):
        return pltpu.make_async_remote_copy(
            src_ref=part_ref.at[src],
            dst_ref=back_ref.at[src],
            send_sem=bs_sem.at[src],
            recv_sem=br_sem.at[src],
            device_id={"img": src // shares, "head": src // reps % heads, "rep": src % reps},
            device_id_type=mesh_ids,
        )

    @pl.loop(0, count)
    def _(t):
        target = (1 - low) * (count - 1 - t) + low * t
        side = jnp.where(own[0] == target // shares, 0, 1)
        chosen = view_ref[side, target % shares]

        @pl.when(target == me)
        def _():
            back_ref[me] = chosen

        @pl.when(target != me)
        def _():
            part_ref[target] = chosen
            b_copy(target).start()

    @pl.loop(1, count)
    def _(step):
        b_arrival((me + step) % count).wait_recv()

    totals = [jnp.zeros(back_ref.shape[1:], jnp.float32) for _ in range(images)]
    for src in range(count):
        one, two = pairs[0, src], pairs[1, src]
        local = jnp.where(
            one // images == i,
            one % images,
            jnp.where(two // images == i, two % images, images),
        )
        block = back_ref[src].astype(jnp.float32)
        for image in range(images):
            totals[image] = totals[image] + jnp.where(local == image, block, 0.0)
    for image in range(images):
        packed = totals[image]
        rest = [packed[channels:, g * extra : (g + 1) * extra] for g in range(strips)]
        total = jnp.concatenate([packed[:channels], jnp.concatenate(rest, axis=0)], axis=1)
        out_ref[:, image, :] = total[: channels - 1] / jnp.maximum(total[channels - 1 :], 1.0)

    for c in range(last + 1):
        for k in order:
            z_copy(source(k), c).wait_send()
        x_copy(c).wait_send()

    @pl.loop(1, count)
    def _(step):
        b_copy((me + step) % count).wait_send()

    for n in range(5):
        for step in range(1, reps):
            weight_remote(n, step).wait_send()


def fused(enc, pairs, w_embed, w_query, w_key, w_value, w_out, wht, gq, gk, spans):
    owners, heads, reps = (lax.axis_size(name) for name in ("img", "head", "rep"))
    images, rows, enc_width = enc.shape
    width = w_embed.shape[1]
    tokens = heads * rows
    part = rows // reps
    channels = wht.shape[0]
    count = owners * heads * reps
    blocks = width // LANES
    bf16 = jnp.bfloat16
    dma = pltpu.SemaphoreType.DMA
    full = pltpu.VMEM((width, width), bf16)
    any_space = pl.BlockSpec(memory_space=pl.ANY)
    vmem = pl.BlockSpec(memory_space=pltpu.VMEM)
    pieces = len(spans)
    return pl.pallas_call(
        functools.partial(fused_kernel, (owners, heads, reps), spans),
        out_shape=jax.ShapeDtypeStruct((channels - 1, images, part), jnp.float32),
        in_specs=[any_space] * 7 + [vmem] * 3,
        out_specs=vmem,
        scratch_shapes=[
            pltpu.VMEM(enc.shape, bf16),
            pltpu.VMEM((enc_width, width), bf16),
            full, full, full, full,
            pltpu.VMEM((owners, rows, width), bf16),
            tuple(pltpu.VMEM((owners, n, width), bf16) for _, n in spans),
            tuple(pltpu.VMEM((2, n, width), bf16) for _, n in spans),
            tuple(pltpu.VMEM((2, n, width), bf16) for _, n in spans),
            pltpu.VMEM((2, tokens, width), bf16),
            pltpu.VMEM((2, tokens, width), bf16),
            pltpu.VMEM((2, blocks, 2 * tokens, LANES), bf16),
            pltpu.VMEM((2, blocks, 2 * tokens, 2 * LANES), bf16),
            pltpu.VMEM((2, tokens, width), bf16),
            pltpu.VMEM((2, blocks, tokens, 2 * LANES), jnp.float32),
            pltpu.VMEM((2, heads * reps, channels + 4, LANES), bf16),
            pltpu.VMEM((count, channels + 4, LANES), bf16),
            pltpu.VMEM((count, channels + 4, LANES), bf16),
            pltpu.SMEM(pairs.shape, jnp.int32),
            dma(()),
            dma(()),
            dma((5,)),
            dma((5, reps)),
            dma((5, reps)),
            dma((owners, pieces)),
            dma((owners, pieces)),
            dma((pieces,)),
            dma((pieces,)),
            dma((count,)),
            dma((count,)),
        ],
        compiler_params=pltpu.CompilerParams(
            collective_id=0, has_side_effects=True, vmem_limit_bytes=56 * 2**20
        ),
        name="decode_views",
    )(pairs, enc, w_embed, w_query, w_key, w_value, w_out, wht, gq, gk).transpose(1, 0, 2)


def cut(rows):
    unit = rows // 9
    spans, offset = [], 0
    for parts in SPAN_PARTS:
        spans.append((offset, parts * unit))
        offset += parts * unit
    return tuple(spans)


def take_each(array, index):
    return jnp.stack(
        [lax.dynamic_index_in_dim(array, index[k], 0, keepdims=False) for k in range(index.shape[0])]
    )


def body(enc, pair_list, w_embed, w_query, w_key, w_value, w_out, w_head, gain_query, gain_key):
    owner_count = lax.axis_size("img")
    head_count = lax.axis_size("head")
    rep_count = lax.axis_size("rep")
    my_owner = lax.axis_index("img")
    my_rep = lax.axis_index("rep")
    img_count, row_count, enc_width = enc.shape
    slot_count = 2 * head_count
    assert slot_count == owner_count
    channels = w_head.shape[1]
    extra = row_count // rep_count - LANES
    fits = 0 < extra and extra % 16 == 0 and channels % 4 == 0 and channels // 4 * extra < LANES
    if fits and head_count == 2 and rep_count == 2 and row_count % 144 == 0 and owner_count % 2 == 0:
        return fused(
            enc, pair_list.T, w_embed, w_query, w_key, w_value, w_out, w_head.T,
            gain_query, gain_key, cut(row_count),
        )
    wht = jnp.pad(w_head.T, ((0, -channels % 16), (0, 0)))
    full_embed, full_query, full_key, full_value, full_out = (
        lax.all_gather(w, "rep", axis=0, tiled=True)
        for w in (w_embed, w_query, w_key, w_value, w_out)
    )
    layout = lax.dynamic_index_in_dim(
        pair_list.reshape(owner_count, head_count, rep_count, 2), my_rep, 2, keepdims=False
    ).reshape(owner_count, slot_count)
    slot_owner = layout // img_count
    mine = slot_owner == my_owner
    pick = jnp.sum(jnp.where(mine, layout % img_count, 0), axis=1)
    group_owner = lax.dynamic_index_in_dim(slot_owner, my_owner, 0, keepdims=False)
    owner_index = group_owner.reshape(head_count, 2).T.reshape(-1)
    slot_of = jnp.sum(
        jnp.where(group_owner[None, :] == jnp.arange(slot_count)[:, None], jnp.arange(slot_count)[None, :], 0),
        axis=1,
    )

    rows = take_each(enc, pick).reshape(-1, enc_width)
    embedded = dot(rows, full_embed).astype(jnp.bfloat16).reshape(owner_count, row_count, -1)
    arrived = lax.all_to_all(embedded, "img", split_axis=0, concat_axis=0, tiled=True)
    grouped = take_each(arrived, owner_index).reshape(2, head_count, row_count, -1)
    spread = lax.all_to_all(grouped, "head", split_axis=1, concat_axis=1, tiled=True)
    x = spread.reshape(2, head_count * row_count, spread.shape[-1])
    weighted = decode(
        x, full_query, full_key, full_value, full_out, wht, gain_query[None], gain_key[None], channels
    )
    back = lax.all_to_all(
        weighted.reshape(2, channels, head_count, row_count),
        "head",
        split_axis=2,
        concat_axis=2,
        tiled=True,
    )
    by_slot = back.transpose(2, 0, 1, 3).reshape(slot_count, channels, row_count)
    received = lax.all_to_all(take_each(by_slot, slot_of), "img", split_axis=0, concat_axis=0, tiled=True)
    chosen = (pick[:, None] == jnp.arange(img_count)[None, :]).astype(jnp.float32)
    totals = jnp.einsum("qi,qxr->ixr", chosen, received, precision=lax.Precision.HIGHEST)
    shares = lax.psum_scatter(totals, "rep", scatter_dimension=2, tiled=True)
    return shares[:, :-1] / jnp.maximum(shares[:, -1:], 1.0)


def solution(mesh):
    in_specs = (
        P(("groups", "img"), "head", None),
        P("groups", None),
        P("rep", None),
        P("rep", None),
        P("rep", None),
        P("rep", None),
        P("rep", None),
        P(),
        P(),
        P(),
    )
    out_specs = P(("groups", "img"), None, ("head", "rep"))
    return jax.shard_map(body, mesh=mesh, in_specs=in_specs, out_specs=out_specs, check_vma=False)
```

```python
import functools
import math

import jax
import jax.numpy as jnp
from jax import lax
from jax.experimental import pallas as pl
from jax.experimental.pallas import tpu as pltpu
from jax.sharding import PartitionSpec as P

HEAD_DIM = 64
NORM_EPSILON = 1e-06
LANES = 128
SPAN_PARTS = (1,) * 9
GROUPS = (4, 7, 9)
QUOTA = 2
AHEAD = 2
UNROLL = 3
VALUE_SCALE = 512.0
QUERY_SCALE = HEAD_DIM**-0.5 * math.log2(math.e)


def dot(left_side, right_side):
    return jnp.dot(left_side, right_side, preferred_element_type=jnp.float32)


def dot_nt(left_side, right_side):
    return lax.dot_general(
        left_side, right_side, (((1,), (1,)), ((), ())), preferred_element_type=jnp.float32
    )


def project_rows(rows, gq, gk, wq_ref, wk_ref, wv_ref):
    widened = rows.astype(jnp.float32)
    center = widened - jnp.mean(widened, axis=-1, keepdims=True)
    spread = jnp.mean(center * center, axis=-1, keepdims=True)
    base = center * lax.rsqrt(spread + NORM_EPSILON)
    query_in = (base * gq).astype(jnp.bfloat16)
    key_in = (base * gk).astype(jnp.bfloat16)
    queries = (dot(query_in, wq_ref[...]) * QUERY_SCALE).astype(jnp.bfloat16)
    keys = dot(key_in, wk_ref[...]).astype(jnp.bfloat16)
    values = (dot(key_in, wv_ref[...]) * (1.0 / VALUE_SCALE)).astype(jnp.bfloat16)
    return queries, keys, values


def decode_kernel(
    x_ref, wq_ref, wk_ref, wv_ref, wo_ref, wh_ref, gq_ref, gk_ref, out_ref, q_ref, k_ref, v_ref, att_ref
):
    tokens, width = x_ref.shape[1:]
    half = tokens // 2
    gq, gk = gq_ref[...], gk_ref[...]

    @pl.loop(0, 4)
    def _(step):
        side = step // 2
        rows = pl.ds(pl.multiple_of((step % 2) * half, half), half)
        queries, keys, values = project_rows(
            x_ref[side, rows, :], gq, gk, wq_ref, wk_ref, wv_ref
        )
        q_ref[side, rows, :] = queries
        k_ref[side, rows, :] = keys
        v_ref[side, rows, :] = values

    blocks = width // LANES

    @pl.loop(0, 2 * blocks)
    def _(step):
        side = step // blocks
        cols = pl.ds(pl.multiple_of(step % blocks * LANES, LANES), LANES)
        att_ref[side, :, cols] = attend_block(
            q_ref[side, :, cols], k_ref[1 - side, :, cols], v_ref[1 - side, :, cols]
        )

    @pl.loop(0, 2)
    def _(side):
        out_ref[side] = finish(x_ref[side], att_ref[side], wo_ref, wh_ref[...], out_ref.shape[1])


def decode(x, wq, wk, wv, wo, wht, gq, gk, channels):
    tokens, width = x.shape[1:]
    scratch = pltpu.VMEM((2, tokens, width), jnp.bfloat16)
    return pl.pallas_call(
        decode_kernel,
        out_shape=jax.ShapeDtypeStruct((2, channels, tokens), jnp.float32),
        scratch_shapes=[scratch] * 4,
        compiler_params=pltpu.CompilerParams(vmem_limit_bytes=48 * 2**20),
        name="decode",
    )(x, wq, wk, wv, wo, wht, gq, gk)


def attend_block(q, k, v):
    lane = lax.broadcasted_iota(jnp.int32, q.shape, 1)
    out = None
    for sub in range(LANES // HEAD_DIM):
        mine = (lane >= sub * HEAD_DIM) & (lane < (sub + 1) * HEAD_DIM)
        scores = dot_nt(jnp.where(mine, q, jnp.zeros_like(q)), k)
        weights = jnp.exp2(scores)
        inverse = 1.0 / jnp.sum(weights, axis=1, keepdims=True)
        probabilities = (weights * inverse).astype(jnp.bfloat16)
        part = dot(probabilities, v) * VALUE_SCALE
        out = part if out is None else jnp.where(mine, part, out)
    return out.astype(jnp.bfloat16)


def finish(own, attended, wo_ref, wh_rows, channels):
    residual = (own.astype(jnp.float32) + dot(attended, wo_ref[...])).astype(jnp.bfloat16)
    decoded = dot_nt(wh_rows, residual)
    last = decoded[channels - 1 : channels]
    confidence = 1.0 + jnp.maximum(last, 0.0) + jnp.log1p(jnp.exp(-jnp.abs(last)))
    row = lax.broadcasted_iota(jnp.int32, (channels, decoded.shape[1]), 0)
    return jnp.where(row == channels - 1, confidence, decoded[:channels] * confidence)


def fused_kernel(
    sizes, spans, pairs_hbm, enc_hbm, we_hbm, wq_hbm, wk_hbm, wv_hbm, wo_hbm, wh_hbm, gq_hbm, gk_hbm, out_ref,
    enc_ref, we_ref, wq_ref, wk_ref, wv_ref, wo_ref, send_ref, land_refs, xs_refs, xr_refs,
    emb_ref, q_ref, k_ref, v_ref, att_ref, sum_ref, view_ref, part_ref, back_ref, wh_ref, gq_ref, gk_ref, pairs,
    small_sem, pair_sem, enc_sem, wl_sem, ws_sem, wr_sem, zs_sem, zr_sem, xs_sem, xr_sem, bs_sem, br_sem,
):
    owners, heads, reps = sizes
    i, h, r = lax.axis_index("img"), lax.axis_index("head"), lax.axis_index("rep")
    images, rows = enc_ref.shape[:2]
    width = emb_ref.shape[2]
    blocks = width // LANES
    mesh_ids = pl.DeviceIdType.MESH
    count = owners * heads * reps
    me = (i * heads + h) * reps + r
    peer = (i * heads + (1 - h)) * reps + r

    barrier = pltpu.get_barrier_semaphore()

    neighbours = [{"img": (i + step) % owners} for step in range(1, owners)]
    neighbours += [{"head": 1 - h}, {"rep": 1 - r}]
    for neighbour in neighbours:
        pl.semaphore_signal(barrier, inc=1, device_id=neighbour, device_id_type=mesh_ids)
    pairs_copy = pltpu.make_async_copy(pairs_hbm, pairs, pair_sem)
    pairs_copy.start()
    weights = (
        (we_hbm, we_ref), (wk_hbm, wk_ref), (wv_hbm, wv_ref), (wq_hbm, wq_ref), (wo_hbm, wo_ref)
    )

    def place(n, rep):
        half, full = weights[n]
        depth = half.shape[0]
        return full.at[pl.ds(pl.multiple_of(rep * depth, depth), depth)]

    def weight_local(n):
        return pltpu.make_async_copy(weights[n][0], place(n, r), wl_sem.at[n])

    def weight_remote(n, step):
        return pltpu.make_async_remote_copy(
            src_ref=weights[n][0],
            dst_ref=place(n, r),
            send_sem=ws_sem.at[n, step],
            recv_sem=wr_sem.at[n, step],
            device_id={"rep": (r + step) % reps},
            device_id_type=mesh_ids,
        )

    weight_local(0).start()
    enc_copy = pltpu.make_async_copy(enc_hbm, enc_ref, enc_sem)
    enc_copy.start()
    for n in range(1, 5):
        weight_local(n).start()
    small = [
        pltpu.make_async_copy(source_ref, target_ref, small_sem.at[n])
        for n, (source_ref, target_ref) in enumerate(((wh_hbm, wh_ref), (gq_hbm, gq_ref), (gk_hbm, gk_ref)))
    ]
    for copy in small:
        copy.start()

    pl.semaphore_wait(barrier, len(neighbours))
    for step in range(1, reps):
        weight_remote(0, step).start()

    def weight_wait(n):
        weight_local(n).wait()
        for step in range(1, reps):
            weight_remote(n, step).wait_recv()

    middle = owners // 2
    low = i // middle

    def source(k):
        base = (low + k // middle) % 2 * middle
        return base + (i % middle + k) % middle

    order = list(range(middle, owners)) + list(range(1, middle))

    def z_copy(d, c):
        offset, n = spans[c]
        return pltpu.make_async_remote_copy(
            src_ref=send_ref.at[d, pl.ds(offset, n)],
            dst_ref=land_refs[c].at[i],
            send_sem=zs_sem.at[d, c],
            recv_sem=zr_sem.at[i, c],
            device_id={"img": d},
            device_id_type=mesh_ids,
        )

    def z_arrival(a, c):
        offset, n = spans[c]
        return pltpu.make_async_remote_copy(
            src_ref=send_ref.at[a, pl.ds(offset, n)],
            dst_ref=land_refs[c].at[a],
            send_sem=zs_sem.at[a, c],
            recv_sem=zr_sem.at[a, c],
            device_id={"img": a},
            device_id_type=mesh_ids,
        )

    def x_copy(c):
        return pltpu.make_async_remote_copy(
            src_ref=xs_refs[c],
            dst_ref=xr_refs[c],
            send_sem=xs_sem.at[c],
            recv_sem=xr_sem.at[c],
            device_id={"head": 1 - h},
            device_id_type=mesh_ids,
        )

    pairs_copy.wait()
    enc_copy.wait()
    weight_wait(0)

    def pick_for(d):
        pick = 0
        for head in range(heads):
            for side in range(2):
                image = pairs[side, (d * heads + head) * reps + r]
                pick = pick + jnp.where(image // images == i, image % images, 0)
        return pick

    targets = [source(k) for k in order] + [i]
    picks = [pick_for(d) for d in targets]

    for c, (offset, n) in enumerate(spans):
        stacked = jnp.concatenate([enc_ref[pick, pl.ds(offset, n), :] for pick in picks], axis=0)
        embedded = dot(stacked, we_ref[...]).astype(jnp.bfloat16)
        for k, d in enumerate(targets):
            mine = embedded[k * n : (k + 1) * n]
            if k < owners - 1:
                send_ref[d, pl.ds(offset, n), :] = mine
                if c < AHEAD:
                    z_copy(d, c).start()
            else:
                land_refs[c][i] = mine
        if c == 0:
            for w in range(1, 5):
                for step in range(1, reps):
                    weight_remote(w, step).start()

    lane = lax.broadcasted_iota(jnp.int32, (1, LANES), 1)
    first = lane < HEAD_DIM
    for offset, n in spans:
        for sub in range(2):
            ones = jnp.where(first == (sub == 0), 1.0, 0.0).astype(jnp.bfloat16)
            v_ref[:, :, pl.ds(4 * offset + 2 * n * sub, 2 * n), pl.ds(LANES, LANES)] = jnp.broadcast_to(
                ones[None, None], (2, blocks, 2 * n, LANES)
            )

    own = [pairs[side, me] // images for side in range(2)]
    other = [pairs[side, peer] // images for side in range(2)]
    for n in range(1, 4):
        weight_wait(n)
    for copy in small:
        copy.wait()
    gq, gk = gq_ref[...][None], gk_ref[...][None]
    zero = jnp.zeros((), jnp.bfloat16)

    def near_rows(c):
        offset, n = spans[c]
        return pl.ds(pl.multiple_of(h * rows + offset, 16), n)

    def far_rows(c):
        offset, n = spans[c]
        return pl.ds(pl.multiple_of((1 - h) * rows + offset, 16), n)

    def forward(c):
        for k in order:
            z_arrival(source(k), c).wait_recv()
        for side in range(2):
            xs_refs[c][side] = land_refs[c][other[side]]
        x_copy(c).start()

    def project(c):
        offset, n = spans[c]
        x_copy(c).wait_recv()
        parts = []
        for side in range(2):
            parts += [land_refs[c][own[side]], xr_refs[c][side]]
        for side in range(2):
            emb_ref[side, near_rows(c), :] = parts[2 * side]
            emb_ref[side, far_rows(c), :] = parts[2 * side + 1]
        queries, keys, values = project_rows(
            jnp.concatenate(parts, axis=0), gq, gk, wq_ref, wk_ref, wv_ref
        )
        for side in range(2):
            top = 2 * side * n
            q_ref[side, near_rows(c), :] = queries[top : top + n]
            q_ref[side, far_rows(c), :] = queries[top + n : top + 2 * n]
            for blk in range(blocks):
                cols = slice(blk * LANES, (blk + 1) * LANES)
                key, value = keys[top : top + 2 * n, cols], values[top : top + 2 * n, cols]
                for sub in range(2):
                    span = pl.ds(4 * offset + 2 * n * sub, 2 * n)
                    keep = first == (sub == 0)
                    k_ref[side, blk, span, :] = jnp.where(keep, key, zero)
                    v_ref[side, blk, span, pl.ds(0, LANES)] = jnp.where(keep, value, zero)

    def attend(steps, begin, end):
        @pl.loop(begin, end)
        def _(t):
            items = []
            for u in range(UNROLL):
                place = t * UNROLL + u
                for step in steps:
                    items.append((place // blocks, place % blocks, step))

            def lanes(blk):
                return pl.ds(pl.multiple_of(blk * LANES, LANES), LANES)

            def score(item):
                side, blk, (pieces, keys, _, _) = item
                queries = [q_ref[side, pl.ds(start, n), lanes(blk)] for start, n in pieces]
                joined = queries[0] if len(queries) == 1 else jnp.concatenate(queries, axis=0)
                return dot_nt(joined, k_ref[1 - side, blk, keys])

            scores = score(items[0])
            for place, item in enumerate(items):
                later = score(items[place + 1]) if place + 1 < len(items) else None
                side, blk, (pieces, keys, adds, ends) = item
                sums = dot(jnp.exp2(scores).astype(jnp.bfloat16), v_ref[1 - side, blk, keys])
                top = 0
                for start, n in pieces:
                    rows_here = pl.ds(start, n)
                    mine = sums[top : top + n]
                    top += n
                    if adds:
                        mine = mine + sum_ref[side, blk, rows_here]
                    if ends:
                        att_ref[side, rows_here, lanes(blk)] = (
                            mine[:, :LANES] * (1.0 / mine[:, LANES:]) * VALUE_SCALE
                        ).astype(jnp.bfloat16)
                    else:
                        sum_ref[side, blk, rows_here] = mine
                scores = later

    def old_steps(g):
        low_row, high_row = edges[g], edges[g + 1]
        ends = g == len(GROUPS) - 1
        return [
            (((head * rows, low_row),), pl.ds(4 * low_row, 4 * (high_row - low_row)), True, ends)
            for head in range(heads)
        ]

    def new_steps(g):
        low_row, high_row = edges[g], edges[g + 1]
        ends = g == len(GROUPS) - 1
        pieces = tuple((head * rows + low_row, high_row - low_row) for head in range(heads))
        if high_row - low_row > 128:
            return [((piece,), pl.ds(0, 4 * high_row), False, ends) for piece in pieces]
        return [(pieces, pl.ds(0, 4 * high_row), False, ends)]

    last = len(spans) - 1
    edges = [0] + [sum(spans[g - 1]) for g in GROUPS]
    turns = 2 * blocks // UNROLL
    ready = []
    for c in range(last + 1):
        forward(c)
        if c + AHEAD <= last:
            for k in order:
                z_copy(source(k), c + AHEAD).start()
        if c > 0:
            project(c - 1)
        if c in GROUPS:
            g = GROUPS.index(c)
            ready += [((old_steps(g) if g else []) + new_steps(g), turn) for turn in range(turns)]
        for steps, turn in ready[:QUOTA]:
            attend(steps, turn, turn + 1)
        ready = ready[QUOTA:]
    for steps, turn in ready:
        attend(steps, turn, turn + 1)
    project(last)
    attend(old_steps(len(GROUPS) - 1) + new_steps(len(GROUPS) - 1), 0, turns)

    weight_wait(4)
    shares = heads * reps
    channels = out_ref.shape[0] + 1
    part = out_ref.shape[2]
    wh_rows = wh_ref[...]
    extra = part - LANES
    strips = channels // 4
    order_rows = [(share * part, LANES) for share in range(shares)]
    order_rows += [(share * part + LANES, extra) for share in range(shares)]

    def arrange(ref, side):
        return jnp.concatenate([ref[side, pl.ds(start, n), :] for start, n in order_rows], axis=0)

    for side in range(2):
        weighted = finish(arrange(emb_ref, side), arrange(att_ref, side), wo_ref, wh_rows, channels)
        for share in range(shares):
            left = shares * LANES + share * extra
            strip = [weighted[4 * g : 4 * g + 4, left : left + extra] for g in range(strips)]
            strip.append(jnp.zeros((4, LANES - strips * extra), jnp.float32))
            packed = jnp.concatenate(
                [weighted[:, share * LANES : (share + 1) * LANES], jnp.concatenate(strip, axis=1)], axis=0
            )
            view_ref[side, share] = packed.astype(view_ref.dtype)

    def b_copy(target):
        return pltpu.make_async_remote_copy(
            src_ref=part_ref.at[target],
            dst_ref=back_ref.at[me],
            send_sem=bs_sem.at[target],
            recv_sem=br_sem.at[me],
            device_id={
                "img": target // shares,
                "head": target // reps % heads,
                "rep": target % reps,
            },
            device_id_type=mesh_ids,
        )

    def b_arrival(src):
        return pltpu.make_async_remote_copy(
            src_ref=part_ref.at[src],
            dst_ref=back_ref.at[src],
            send_sem=bs_sem.at[src],
            recv_sem=br_sem.at[src],
            device_id={"img": src // shares, "head": src // reps % heads, "rep": src % reps},
            device_id_type=mesh_ids,
        )

    mine_share = h * reps + r
    for d in [source(k) for k in order]:
        side = jnp.where(own[0] == d, 0, 1)
        for share in range(shares):
            part_ref[d * shares + share] = view_ref[side, share]
            b_copy(d * shares + share).start()
    near_side = jnp.where(own[0] == i, 0, 1)
    for step in range(1, shares):
        share = (mine_share + step) % shares
        part_ref[i * shares + share] = view_ref[near_side, share]
        b_copy(i * shares + share).start()
    back_ref[me] = view_ref[near_side, mine_share]

    for c in range(last + 1):
        for k in order:
            z_copy(source(k), c).wait_send()
        x_copy(c).wait_send()
    for n in range(5):
        for step in range(1, reps):
            weight_remote(n, step).wait_send()

    for step in range(1, count):
        b_arrival((me + step) % count).wait_recv()

    totals = [jnp.zeros(back_ref.shape[1:], jnp.float32) for _ in range(images)]
    for src in range(count):
        one, two = pairs[0, src], pairs[1, src]
        local = jnp.where(
            one // images == i,
            one % images,
            jnp.where(two // images == i, two % images, images),
        )
        block = back_ref[src].astype(jnp.float32)
        for image in range(images):
            totals[image] = totals[image] + jnp.where(local == image, block, 0.0)
    for image in range(images):
        packed = totals[image]
        rest = [packed[channels:, g * extra : (g + 1) * extra] for g in range(strips)]
        total = jnp.concatenate([packed[:channels], jnp.concatenate(rest, axis=0)], axis=1)
        out_ref[:, image, :] = total[: channels - 1] / jnp.maximum(total[channels - 1 :], 1.0)

    for step in range(1, count):
        b_copy((me + step) % count).wait_send()


def fused(enc, pairs, w_embed, w_query, w_key, w_value, w_out, wht, gq, gk, spans):
    owners, heads, reps = (lax.axis_size(name) for name in ("img", "head", "rep"))
    images, rows, enc_width = enc.shape
    width = w_embed.shape[1]
    tokens = heads * rows
    part = rows // reps
    channels = wht.shape[0]
    count = owners * heads * reps
    blocks = width // LANES
    bf16 = jnp.bfloat16
    dma = pltpu.SemaphoreType.DMA
    full = pltpu.VMEM((width, width), bf16)
    any_space = pl.BlockSpec(memory_space=pl.ANY)
    vmem = pl.BlockSpec(memory_space=pltpu.VMEM)
    pieces = len(spans)
    return pl.pallas_call(
        functools.partial(fused_kernel, (owners, heads, reps), spans),
        out_shape=jax.ShapeDtypeStruct((channels - 1, images, part), jnp.float32),
        in_specs=[any_space] * 10,
        out_specs=vmem,
        scratch_shapes=[
            pltpu.VMEM(enc.shape, bf16),
            pltpu.VMEM((enc_width, width), bf16),
            full, full, full, full,
            pltpu.VMEM((owners, rows, width), bf16),
            tuple(pltpu.VMEM((owners, n, width), bf16) for _, n in spans),
            tuple(pltpu.VMEM((2, n, width), bf16) for _, n in spans),
            tuple(pltpu.VMEM((2, n, width), bf16) for _, n in spans),
            pltpu.VMEM((2, tokens, width), bf16),
            pltpu.VMEM((2, tokens, width), bf16),
            pltpu.VMEM((2, blocks, 2 * tokens, LANES), bf16),
            pltpu.VMEM((2, blocks, 2 * tokens, 2 * LANES), bf16),
            pltpu.VMEM((2, tokens, width), bf16),
            pltpu.VMEM((2, blocks, tokens, 2 * LANES), jnp.float32),
            pltpu.VMEM((2, heads * reps, channels + 4, LANES), bf16),
            pltpu.VMEM((count, channels + 4, LANES), bf16),
            pltpu.VMEM((count, channels + 4, LANES), bf16),
            pltpu.VMEM(wht.shape, bf16),
            pltpu.VMEM(gq.shape, jnp.float32),
            pltpu.VMEM(gk.shape, jnp.float32),
            pltpu.SMEM(pairs.shape, jnp.int32),
            dma((3,)),
            dma(()),
            dma(()),
            dma((5,)),
            dma((5, reps)),
            dma((5, reps)),
            dma((owners, pieces)),
            dma((owners, pieces)),
            dma((pieces,)),
            dma((pieces,)),
            dma((count,)),
            dma((count,)),
        ],
        compiler_params=pltpu.CompilerParams(
            collective_id=0, has_side_effects=True, vmem_limit_bytes=56 * 2**20
        ),
        name="decode_views",
    )(pairs, enc, w_embed, w_query, w_key, w_value, w_out, wht, gq, gk).transpose(1, 0, 2)


def cut(rows):
    unit = rows // 9
    spans, offset = [], 0
    for parts in SPAN_PARTS:
        spans.append((offset, parts * unit))
        offset += parts * unit
    return tuple(spans)


def take_each(array, index):
    return jnp.stack(
        [lax.dynamic_index_in_dim(array, index[k], 0, keepdims=False) for k in range(index.shape[0])]
    )


def body(enc, pair_list, w_embed, w_query, w_key, w_value, w_out, w_head, gain_query, gain_key):
    owner_count = lax.axis_size("img")
    head_count = lax.axis_size("head")
    rep_count = lax.axis_size("rep")
    my_owner = lax.axis_index("img")
    my_rep = lax.axis_index("rep")
    img_count, row_count, enc_width = enc.shape
    slot_count = 2 * head_count
    assert slot_count == owner_count
    channels = w_head.shape[1]
    extra = row_count // rep_count - LANES
    fits = 0 < extra and extra % 16 == 0 and channels % 4 == 0 and channels // 4 * extra < LANES
    if fits and head_count == 2 and rep_count == 2 and row_count % 144 == 0 and owner_count % 2 == 0:
        return fused(
            enc, pair_list.T, w_embed, w_query, w_key, w_value, w_out, w_head.T,
            gain_query, gain_key, cut(row_count),
        )
    wht = jnp.pad(w_head.T, ((0, -channels % 16), (0, 0)))
    full_embed, full_query, full_key, full_value, full_out = (
        lax.all_gather(w, "rep", axis=0, tiled=True)
        for w in (w_embed, w_query, w_key, w_value, w_out)
    )
    layout = lax.dynamic_index_in_dim(
        pair_list.reshape(owner_count, head_count, rep_count, 2), my_rep, 2, keepdims=False
    ).reshape(owner_count, slot_count)
    slot_owner = layout // img_count
    mine = slot_owner == my_owner
    pick = jnp.sum(jnp.where(mine, layout % img_count, 0), axis=1)
    group_owner = lax.dynamic_index_in_dim(slot_owner, my_owner, 0, keepdims=False)
    owner_index = group_owner.reshape(head_count, 2).T.reshape(-1)
    slot_of = jnp.sum(
        jnp.where(group_owner[None, :] == jnp.arange(slot_count)[:, None], jnp.arange(slot_count)[None, :], 0),
        axis=1,
    )

    rows = take_each(enc, pick).reshape(-1, enc_width)
    embedded = dot(rows, full_embed).astype(jnp.bfloat16).reshape(owner_count, row_count, -1)
    arrived = lax.all_to_all(embedded, "img", split_axis=0, concat_axis=0, tiled=True)
    grouped = take_each(arrived, owner_index).reshape(2, head_count, row_count, -1)
    spread = lax.all_to_all(grouped, "head", split_axis=1, concat_axis=1, tiled=True)
    x = spread.reshape(2, head_count * row_count, spread.shape[-1])
    weighted = decode(
        x, full_query, full_key, full_value, full_out, wht, gain_query[None], gain_key[None], channels
    )
    back = lax.all_to_all(
        weighted.reshape(2, channels, head_count, row_count),
        "head",
        split_axis=2,
        concat_axis=2,
        tiled=True,
    )
    by_slot = back.transpose(2, 0, 1, 3).reshape(slot_count, channels, row_count)
    received = lax.all_to_all(take_each(by_slot, slot_of), "img", split_axis=0, concat_axis=0, tiled=True)
    chosen = (pick[:, None] == jnp.arange(img_count)[None, :]).astype(jnp.float32)
    totals = jnp.einsum("qi,qxr->ixr", chosen, received, precision=lax.Precision.HIGHEST)
    shares = lax.psum_scatter(totals, "rep", scatter_dimension=2, tiled=True)
    return shares[:, :-1] / jnp.maximum(shares[:, -1:], 1.0)


def solution(mesh):
    in_specs = (
        P(("groups", "img"), "head", None),
        P("groups", None),
        P("rep", None),
        P("rep", None),
        P("rep", None),
        P("rep", None),
        P("rep", None),
        P(),
        P(),
        P(),
    )
    out_specs = P(("groups", "img"), None, ("head", "rep"))
    return jax.shard_map(body, mesh=mesh, in_specs=in_specs, out_specs=out_specs, check_vma=False)
```

```python
import functools
import math

import jax
import jax.numpy as jnp
from jax import lax
from jax.experimental import pallas as pl
from jax.experimental.pallas import tpu as pltpu
from jax.sharding import PartitionSpec as P

HEAD_DIM = 64
NORM_EPSILON = 1e-06
LANES = 128
SPAN_PARTS = (1,) * 9
GROUPS = (5, 7, 9)
QUOTA = 2
AHEAD = 2
UNROLL = 3
VALUE_SCALE = 512.0
QUERY_SCALE = HEAD_DIM**-0.5 * math.log2(math.e)


def dot(left_side, right_side):
    return jnp.dot(left_side, right_side, preferred_element_type=jnp.float32)


def dot_nt(left_side, right_side):
    return lax.dot_general(
        left_side, right_side, (((1,), (1,)), ((), ())), preferred_element_type=jnp.float32
    )


def project_rows(rows, gq, gk, wq_ref, wk_ref, wv_ref):
    widened = rows.astype(jnp.float32)
    center = widened - jnp.mean(widened, axis=-1, keepdims=True)
    spread = jnp.mean(center * center, axis=-1, keepdims=True)
    base = center * lax.rsqrt(spread + NORM_EPSILON)
    query_in = (base * gq).astype(jnp.bfloat16)
    key_in = (base * gk).astype(jnp.bfloat16)
    queries = (dot(query_in, wq_ref[...]) * QUERY_SCALE).astype(jnp.bfloat16)
    keys = dot(key_in, wk_ref[...]).astype(jnp.bfloat16)
    values = (dot(key_in, wv_ref[...]) * (1.0 / VALUE_SCALE)).astype(jnp.bfloat16)
    return queries, keys, values


def decode_kernel(
    x_ref, wq_ref, wk_ref, wv_ref, wo_ref, wh_ref, gq_ref, gk_ref, out_ref, q_ref, k_ref, v_ref, att_ref
):
    tokens, width = x_ref.shape[1:]
    half = tokens // 2
    gq, gk = gq_ref[...], gk_ref[...]

    @pl.loop(0, 4)
    def _(step):
        side = step // 2
        rows = pl.ds(pl.multiple_of((step % 2) * half, half), half)
        queries, keys, values = project_rows(
            x_ref[side, rows, :], gq, gk, wq_ref, wk_ref, wv_ref
        )
        q_ref[side, rows, :] = queries
        k_ref[side, rows, :] = keys
        v_ref[side, rows, :] = values

    blocks = width // LANES

    @pl.loop(0, 2 * blocks)
    def _(step):
        side = step // blocks
        cols = pl.ds(pl.multiple_of(step % blocks * LANES, LANES), LANES)
        att_ref[side, :, cols] = attend_block(
            q_ref[side, :, cols], k_ref[1 - side, :, cols], v_ref[1 - side, :, cols]
        )

    @pl.loop(0, 2)
    def _(side):
        out_ref[side] = finish(x_ref[side], att_ref[side], wo_ref, wh_ref[...], out_ref.shape[1])


def decode(x, wq, wk, wv, wo, wht, gq, gk, channels):
    tokens, width = x.shape[1:]
    scratch = pltpu.VMEM((2, tokens, width), jnp.bfloat16)
    return pl.pallas_call(
        decode_kernel,
        out_shape=jax.ShapeDtypeStruct((2, channels, tokens), jnp.float32),
        scratch_shapes=[scratch] * 4,
        compiler_params=pltpu.CompilerParams(vmem_limit_bytes=48 * 2**20),
        name="decode",
    )(x, wq, wk, wv, wo, wht, gq, gk)


def attend_block(q, k, v):
    lane = lax.broadcasted_iota(jnp.int32, q.shape, 1)
    out = None
    for sub in range(LANES // HEAD_DIM):
        mine = (lane >= sub * HEAD_DIM) & (lane < (sub + 1) * HEAD_DIM)
        scores = dot_nt(jnp.where(mine, q, jnp.zeros_like(q)), k)
        weights = jnp.exp2(scores)
        inverse = 1.0 / jnp.sum(weights, axis=1, keepdims=True)
        probabilities = (weights * inverse).astype(jnp.bfloat16)
        part = dot(probabilities, v) * VALUE_SCALE
        out = part if out is None else jnp.where(mine, part, out)
    return out.astype(jnp.bfloat16)


def finish(own, attended, wo_ref, wh_rows, channels):
    residual = (own.astype(jnp.float32) + dot(attended, wo_ref[...])).astype(jnp.bfloat16)
    decoded = dot_nt(wh_rows, residual)
    last = decoded[channels - 1 : channels]
    confidence = 1.0 + jnp.maximum(last, 0.0) + jnp.log1p(jnp.exp(-jnp.abs(last)))
    row = lax.broadcasted_iota(jnp.int32, (channels, decoded.shape[1]), 0)
    return jnp.where(row == channels - 1, confidence, decoded[:channels] * confidence)


def fused_kernel(
    sizes, spans, pairs_hbm, enc_hbm, we_hbm, wq_hbm, wk_hbm, wv_hbm, wo_hbm, wh_hbm, gq_hbm, gk_hbm, out_ref,
    enc_ref, we_ref, wq_ref, wk_ref, wv_ref, wo_ref, send_ref, land_refs, xs_refs, xr_refs,
    emb_ref, q_ref, k_ref, v_ref, att_ref, sum_ref, view_ref, part_ref, back_ref, wh_ref, gq_ref, gk_ref, pairs,
    small_sem, pair_sem, enc_sem, wl_sem, ws_sem, wr_sem, zs_sem, zr_sem, xs_sem, xr_sem, bs_sem, br_sem,
):
    owners, heads, reps = sizes
    i, h, r = lax.axis_index("img"), lax.axis_index("head"), lax.axis_index("rep")
    images, rows = enc_ref.shape[:2]
    width = emb_ref.shape[2]
    blocks = width // LANES
    mesh_ids = pl.DeviceIdType.MESH
    count = owners * heads * reps
    me = (i * heads + h) * reps + r
    peer = (i * heads + (1 - h)) * reps + r

    barrier = pltpu.get_barrier_semaphore()

    neighbours = [{"img": (i + step) % owners} for step in range(1, owners)]
    neighbours += [{"head": 1 - h}, {"rep": 1 - r}]
    for neighbour in neighbours:
        pl.semaphore_signal(barrier, inc=1, device_id=neighbour, device_id_type=mesh_ids)
    pairs_copy = pltpu.make_async_copy(pairs_hbm, pairs, pair_sem)
    pairs_copy.start()
    weights = (
        (we_hbm, we_ref), (wk_hbm, wk_ref), (wv_hbm, wv_ref), (wq_hbm, wq_ref), (wo_hbm, wo_ref)
    )

    def place(n, rep):
        half, full = weights[n]
        depth = half.shape[0]
        return full.at[pl.ds(pl.multiple_of(rep * depth, depth), depth)]

    def weight_local(n):
        return pltpu.make_async_copy(weights[n][0], place(n, r), wl_sem.at[n])

    def weight_remote(n, step):
        return pltpu.make_async_remote_copy(
            src_ref=weights[n][0],
            dst_ref=place(n, r),
            send_sem=ws_sem.at[n, step],
            recv_sem=wr_sem.at[n, step],
            device_id={"rep": (r + step) % reps},
            device_id_type=mesh_ids,
        )

    weight_local(0).start()
    enc_copy = pltpu.make_async_copy(enc_hbm, enc_ref, enc_sem)
    enc_copy.start()
    for n in range(1, 5):
        weight_local(n).start()
    small = [
        pltpu.make_async_copy(source_ref, target_ref, small_sem.at[n])
        for n, (source_ref, target_ref) in enumerate(((wh_hbm, wh_ref), (gq_hbm, gq_ref), (gk_hbm, gk_ref)))
    ]
    for copy in small:
        copy.start()

    pl.semaphore_wait(barrier, len(neighbours))
    for step in range(1, reps):
        weight_remote(0, step).start()

    def weight_wait(n):
        weight_local(n).wait()
        for step in range(1, reps):
            weight_remote(n, step).wait_recv()

    middle = owners // 2
    low = i // middle

    def source(k):
        base = (low + k // middle) % 2 * middle
        return base + (i % middle + k) % middle

    order = list(range(middle, owners)) + list(range(1, middle))

    def z_copy(d, c):
        offset, n = spans[c]
        return pltpu.make_async_remote_copy(
            src_ref=send_ref.at[d, pl.ds(offset, n)],
            dst_ref=land_refs[c].at[i],
            send_sem=zs_sem.at[d, c],
            recv_sem=zr_sem.at[i, c],
            device_id={"img": d},
            device_id_type=mesh_ids,
        )

    def z_arrival(a, c):
        offset, n = spans[c]
        return pltpu.make_async_remote_copy(
            src_ref=send_ref.at[a, pl.ds(offset, n)],
            dst_ref=land_refs[c].at[a],
            send_sem=zs_sem.at[a, c],
            recv_sem=zr_sem.at[a, c],
            device_id={"img": a},
            device_id_type=mesh_ids,
        )

    def x_copy(c):
        return pltpu.make_async_remote_copy(
            src_ref=xs_refs[c],
            dst_ref=xr_refs[c],
            send_sem=xs_sem.at[c],
            recv_sem=xr_sem.at[c],
            device_id={"head": 1 - h},
            device_id_type=mesh_ids,
        )

    pairs_copy.wait()
    enc_copy.wait()
    weight_wait(0)

    def pick_for(d):
        pick = 0
        for head in range(heads):
            for side in range(2):
                image = pairs[side, (d * heads + head) * reps + r]
                pick = pick + jnp.where(image // images == i, image % images, 0)
        return pick

    targets = [source(k) for k in order] + [i]
    picks = [pick_for(d) for d in targets]

    for c, (offset, n) in enumerate(spans):
        stacked = jnp.concatenate([enc_ref[pick, pl.ds(offset, n), :] for pick in picks], axis=0)
        embedded = dot(stacked, we_ref[...]).astype(jnp.bfloat16)
        for k, d in enumerate(targets):
            mine = embedded[k * n : (k + 1) * n]
            if k < owners - 1:
                send_ref[d, pl.ds(offset, n), :] = mine
                if c < AHEAD:
                    z_copy(d, c).start()
            else:
                land_refs[c][i] = mine
        if c == 0:
            for w in range(1, 5):
                for step in range(1, reps):
                    weight_remote(w, step).start()

    lane = lax.broadcasted_iota(jnp.int32, (1, LANES), 1)
    first = lane < HEAD_DIM
    for offset, n in spans:
        for sub in range(2):
            ones = jnp.where(first == (sub == 0), 1.0, 0.0).astype(jnp.bfloat16)
            v_ref[:, :, pl.ds(4 * offset + 2 * n * sub, 2 * n), pl.ds(LANES, LANES)] = jnp.broadcast_to(
                ones[None, None], (2, blocks, 2 * n, LANES)
            )

    own = [pairs[side, me] // images for side in range(2)]
    other = [pairs[side, peer] // images for side in range(2)]
    for n in range(1, 4):
        weight_wait(n)
    for copy in small:
        copy.wait()
    gq, gk = gq_ref[...][None], gk_ref[...][None]
    zero = jnp.zeros((), jnp.bfloat16)

    def near_rows(c):
        offset, n = spans[c]
        return pl.ds(pl.multiple_of(h * rows + offset, 16), n)

    def far_rows(c):
        offset, n = spans[c]
        return pl.ds(pl.multiple_of((1 - h) * rows + offset, 16), n)

    def forward(c):
        for k in order:
            z_arrival(source(k), c).wait_recv()
        for side in range(2):
            xs_refs[c][side] = land_refs[c][other[side]]
        x_copy(c).start()

    def project(c):
        offset, n = spans[c]
        x_copy(c).wait_recv()
        parts = []
        for side in range(2):
            parts += [land_refs[c][own[side]], xr_refs[c][side]]
        for side in range(2):
            emb_ref[side, near_rows(c), :] = parts[2 * side]
            emb_ref[side, far_rows(c), :] = parts[2 * side + 1]
        queries, keys, values = project_rows(
            jnp.concatenate(parts, axis=0), gq, gk, wq_ref, wk_ref, wv_ref
        )
        for side in range(2):
            top = 2 * side * n
            q_ref[side, near_rows(c), :] = queries[top : top + n]
            q_ref[side, far_rows(c), :] = queries[top + n : top + 2 * n]
            for blk in range(blocks):
                cols = slice(blk * LANES, (blk + 1) * LANES)
                key, value = keys[top : top + 2 * n, cols], values[top : top + 2 * n, cols]
                doubled = jnp.concatenate(
                    [jnp.where(first, key, zero), jnp.where(first, zero, key)], axis=0
                )
                k_ref[side, blk, :, pl.ds(4 * offset, 4 * n)] = doubled.T
                for sub in range(2):
                    span = pl.ds(4 * offset + 2 * n * sub, 2 * n)
                    keep = first == (sub == 0)
                    v_ref[side, blk, span, pl.ds(0, LANES)] = jnp.where(keep, value, zero)

    def attend(steps, begin, end):
        @pl.loop(begin, end)
        def _(t):
            items = []
            for u in range(UNROLL):
                place = t * UNROLL + u
                for step in steps:
                    items.append((place // blocks, place % blocks, step))

            def lanes(blk):
                return pl.ds(pl.multiple_of(blk * LANES, LANES), LANES)

            def score(item):
                side, blk, (pieces, keys, _, _) = item
                queries = [q_ref[side, pl.ds(start, n), lanes(blk)] for start, n in pieces]
                joined = queries[0] if len(queries) == 1 else jnp.concatenate(queries, axis=0)
                return dot(joined, k_ref[1 - side, blk, :, keys])

            scores = score(items[0])
            for place, item in enumerate(items):
                later = score(items[place + 1]) if place + 1 < len(items) else None
                side, blk, (pieces, keys, adds, ends) = item
                sums = dot(jnp.exp2(scores).astype(jnp.bfloat16), v_ref[1 - side, blk, keys])
                top = 0
                for start, n in pieces:
                    rows_here = pl.ds(start, n)
                    mine = sums[top : top + n]
                    top += n
                    if adds:
                        mine = mine + sum_ref[side, blk, rows_here]
                    if ends:
                        att_ref[side, rows_here, lanes(blk)] = (
                            mine[:, :LANES] * (1.0 / mine[:, LANES:]) * VALUE_SCALE
                        ).astype(jnp.bfloat16)
                    else:
                        sum_ref[side, blk, rows_here] = mine
                scores = later

    def old_steps(g):
        low_row, high_row = edges[g], edges[g + 1]
        ends = g == len(GROUPS) - 1
        return [
            (((head * rows, low_row),), pl.ds(4 * low_row, 4 * (high_row - low_row)), True, ends)
            for head in range(heads)
        ]

    def new_steps(g):
        low_row, high_row = edges[g], edges[g + 1]
        ends = g == len(GROUPS) - 1
        pieces = tuple((head * rows + low_row, high_row - low_row) for head in range(heads))
        if high_row - low_row > 128:
            return [((piece,), pl.ds(0, 4 * high_row), False, ends) for piece in pieces]
        return [(pieces, pl.ds(0, 4 * high_row), False, ends)]

    last = len(spans) - 1
    edges = [0] + [sum(spans[g - 1]) for g in GROUPS]
    turns = 2 * blocks // UNROLL
    ready = []
    for c in range(last + 1):
        forward(c)
        if c + AHEAD <= last:
            for k in order:
                z_copy(source(k), c + AHEAD).start()
        if c > 0:
            project(c - 1)
        if c in GROUPS:
            g = GROUPS.index(c)
            ready += [((old_steps(g) if g else []) + new_steps(g), turn) for turn in range(turns)]
        for steps, turn in ready[:QUOTA]:
            attend(steps, turn, turn + 1)
        ready = ready[QUOTA:]
    for steps, turn in ready:
        attend(steps, turn, turn + 1)
    project(last)
    attend(old_steps(len(GROUPS) - 1) + new_steps(len(GROUPS) - 1), 0, turns)

    weight_wait(4)
    shares = heads * reps
    channels = out_ref.shape[0] + 1
    part = out_ref.shape[2]
    wh_rows = wh_ref[...]
    extra = part - LANES
    strips = channels // 4
    order_rows = [(share * part, LANES) for share in range(shares)]
    order_rows += [(share * part + LANES, extra) for share in range(shares)]

    def arrange(ref, side):
        return jnp.concatenate([ref[side, pl.ds(start, n), :] for start, n in order_rows], axis=0)

    for side in range(2):
        weighted = finish(arrange(emb_ref, side), arrange(att_ref, side), wo_ref, wh_rows, channels)
        for share in range(shares):
            left = shares * LANES + share * extra
            strip = [weighted[4 * g : 4 * g + 4, left : left + extra] for g in range(strips)]
            strip.append(jnp.zeros((4, LANES - strips * extra), jnp.float32))
            packed = jnp.concatenate(
                [weighted[:, share * LANES : (share + 1) * LANES], jnp.concatenate(strip, axis=1)], axis=0
            )
            view_ref[side, share] = packed.astype(view_ref.dtype)

    def b_copy(target):
        return pltpu.make_async_remote_copy(
            src_ref=part_ref.at[target],
            dst_ref=back_ref.at[me],
            send_sem=bs_sem.at[target],
            recv_sem=br_sem.at[me],
            device_id={
                "img": target // shares,
                "head": target // reps % heads,
                "rep": target % reps,
            },
            device_id_type=mesh_ids,
        )

    def b_arrival(src):
        return pltpu.make_async_remote_copy(
            src_ref=part_ref.at[src],
            dst_ref=back_ref.at[src],
            send_sem=bs_sem.at[src],
            recv_sem=br_sem.at[src],
            device_id={"img": src // shares, "head": src // reps % heads, "rep": src % reps},
            device_id_type=mesh_ids,
        )

    mine_share = h * reps + r
    for d in [source(k) for k in order]:
        side = jnp.where(own[0] == d, 0, 1)
        for share in range(shares):
            part_ref[d * shares + share] = view_ref[side, share]
            b_copy(d * shares + share).start()
    near_side = jnp.where(own[0] == i, 0, 1)
    for step in range(1, shares):
        share = (mine_share + step) % shares
        part_ref[i * shares + share] = view_ref[near_side, share]
        b_copy(i * shares + share).start()
    back_ref[me] = view_ref[near_side, mine_share]

    for c in range(last + 1):
        for k in order:
            z_copy(source(k), c).wait_send()
        x_copy(c).wait_send()
    for n in range(5):
        for step in range(1, reps):
            weight_remote(n, step).wait_send()

    for step in range(1, count):
        b_arrival((me + step) % count).wait_recv()

    totals = [jnp.zeros(back_ref.shape[1:], jnp.float32) for _ in range(images)]
    for src in range(count):
        one, two = pairs[0, src], pairs[1, src]
        local = jnp.where(
            one // images == i,
            one % images,
            jnp.where(two // images == i, two % images, images),
        )
        block = back_ref[src].astype(jnp.float32)
        for image in range(images):
            totals[image] = totals[image] + jnp.where(local == image, block, 0.0)
    for image in range(images):
        packed = totals[image]
        rest = [packed[channels:, g * extra : (g + 1) * extra] for g in range(strips)]
        total = jnp.concatenate([packed[:channels], jnp.concatenate(rest, axis=0)], axis=1)
        out_ref[:, image, :] = total[: channels - 1] / jnp.maximum(total[channels - 1 :], 1.0)

    for step in range(1, count):
        b_copy((me + step) % count).wait_send()


def fused(enc, pairs, w_embed, w_query, w_key, w_value, w_out, wht, gq, gk, spans):
    owners, heads, reps = (lax.axis_size(name) for name in ("img", "head", "rep"))
    images, rows, enc_width = enc.shape
    width = w_embed.shape[1]
    tokens = heads * rows
    part = rows // reps
    channels = wht.shape[0]
    count = owners * heads * reps
    blocks = width // LANES
    bf16 = jnp.bfloat16
    dma = pltpu.SemaphoreType.DMA
    full = pltpu.VMEM((width, width), bf16)
    any_space = pl.BlockSpec(memory_space=pl.ANY)
    vmem = pl.BlockSpec(memory_space=pltpu.VMEM)
    pieces = len(spans)
    return pl.pallas_call(
        functools.partial(fused_kernel, (owners, heads, reps), spans),
        out_shape=jax.ShapeDtypeStruct((channels - 1, images, part), jnp.float32),
        in_specs=[any_space] * 10,
        out_specs=vmem,
        scratch_shapes=[
            pltpu.VMEM(enc.shape, bf16),
            pltpu.VMEM((enc_width, width), bf16),
            full, full, full, full,
            pltpu.VMEM((owners, rows, width), bf16),
            tuple(pltpu.VMEM((owners, n, width), bf16) for _, n in spans),
            tuple(pltpu.VMEM((2, n, width), bf16) for _, n in spans),
            tuple(pltpu.VMEM((2, n, width), bf16) for _, n in spans),
            pltpu.VMEM((2, tokens, width), bf16),
            pltpu.VMEM((2, tokens, width), bf16),
            pltpu.VMEM((2, blocks, LANES, 2 * tokens), bf16),
            pltpu.VMEM((2, blocks, 2 * tokens, 2 * LANES), bf16),
            pltpu.VMEM((2, tokens, width), bf16),
            pltpu.VMEM((2, blocks, tokens, 2 * LANES), jnp.float32),
            pltpu.VMEM((2, heads * reps, channels + 4, LANES), bf16),
            pltpu.VMEM((count, channels + 4, LANES), bf16),
            pltpu.VMEM((count, channels + 4, LANES), bf16),
            pltpu.VMEM(wht.shape, bf16),
            pltpu.VMEM(gq.shape, jnp.float32),
            pltpu.VMEM(gk.shape, jnp.float32),
            pltpu.SMEM(pairs.shape, jnp.int32),
            dma((3,)),
            dma(()),
            dma(()),
            dma((5,)),
            dma((5, reps)),
            dma((5, reps)),
            dma((owners, pieces)),
            dma((owners, pieces)),
            dma((pieces,)),
            dma((pieces,)),
            dma((count,)),
            dma((count,)),
        ],
        compiler_params=pltpu.CompilerParams(
            collective_id=0, has_side_effects=True, vmem_limit_bytes=56 * 2**20
        ),
        name="decode_views",
    )(pairs, enc, w_embed, w_query, w_key, w_value, w_out, wht, gq, gk).transpose(1, 0, 2)


def cut(rows):
    unit = rows // 9
    spans, offset = [], 0
    for parts in SPAN_PARTS:
        spans.append((offset, parts * unit))
        offset += parts * unit
    return tuple(spans)


def take_each(array, index):
    return jnp.stack(
        [lax.dynamic_index_in_dim(array, index[k], 0, keepdims=False) for k in range(index.shape[0])]
    )


def body(enc, pair_list, w_embed, w_query, w_key, w_value, w_out, w_head, gain_query, gain_key):
    owner_count = lax.axis_size("img")
    head_count = lax.axis_size("head")
    rep_count = lax.axis_size("rep")
    my_owner = lax.axis_index("img")
    my_rep = lax.axis_index("rep")
    img_count, row_count, enc_width = enc.shape
    slot_count = 2 * head_count
    assert slot_count == owner_count
    channels = w_head.shape[1]
    extra = row_count // rep_count - LANES
    fits = 0 < extra and extra % 16 == 0 and channels % 4 == 0 and channels // 4 * extra < LANES
    if fits and head_count == 2 and rep_count == 2 and row_count % 144 == 0 and owner_count % 2 == 0:
        return fused(
            enc, pair_list.T, w_embed, w_query, w_key, w_value, w_out, w_head.T,
            gain_query, gain_key, cut(row_count),
        )
    wht = jnp.pad(w_head.T, ((0, -channels % 16), (0, 0)))
    full_embed, full_query, full_key, full_value, full_out = (
        lax.all_gather(w, "rep", axis=0, tiled=True)
        for w in (w_embed, w_query, w_key, w_value, w_out)
    )
    layout = lax.dynamic_index_in_dim(
        pair_list.reshape(owner_count, head_count, rep_count, 2), my_rep, 2, keepdims=False
    ).reshape(owner_count, slot_count)
    slot_owner = layout // img_count
    mine = slot_owner == my_owner
    pick = jnp.sum(jnp.where(mine, layout % img_count, 0), axis=1)
    group_owner = lax.dynamic_index_in_dim(slot_owner, my_owner, 0, keepdims=False)
    owner_index = group_owner.reshape(head_count, 2).T.reshape(-1)
    slot_of = jnp.sum(
        jnp.where(group_owner[None, :] == jnp.arange(slot_count)[:, None], jnp.arange(slot_count)[None, :], 0),
        axis=1,
    )

    rows = take_each(enc, pick).reshape(-1, enc_width)
    embedded = dot(rows, full_embed).astype(jnp.bfloat16).reshape(owner_count, row_count, -1)
    arrived = lax.all_to_all(embedded, "img", split_axis=0, concat_axis=0, tiled=True)
    grouped = take_each(arrived, owner_index).reshape(2, head_count, row_count, -1)
    spread = lax.all_to_all(grouped, "head", split_axis=1, concat_axis=1, tiled=True)
    x = spread.reshape(2, head_count * row_count, spread.shape[-1])
    weighted = decode(
        x, full_query, full_key, full_value, full_out, wht, gain_query[None], gain_key[None], channels
    )
    back = lax.all_to_all(
        weighted.reshape(2, channels, head_count, row_count),
        "head",
        split_axis=2,
        concat_axis=2,
        tiled=True,
    )
    by_slot = back.transpose(2, 0, 1, 3).reshape(slot_count, channels, row_count)
    received = lax.all_to_all(take_each(by_slot, slot_of), "img", split_axis=0, concat_axis=0, tiled=True)
    chosen = (pick[:, None] == jnp.arange(img_count)[None, :]).astype(jnp.float32)
    totals = jnp.einsum("qi,qxr->ixr", chosen, received, precision=lax.Precision.HIGHEST)
    shares = lax.psum_scatter(totals, "rep", scatter_dimension=2, tiled=True)
    return shares[:, :-1] / jnp.maximum(shares[:, -1:], 1.0)


def solution(mesh):
    in_specs = (
        P(("groups", "img"), "head", None),
        P("groups", None),
        P("rep", None),
        P("rep", None),
        P("rep", None),
        P("rep", None),
        P("rep", None),
        P(),
        P(),
        P(),
    )
    out_specs = P(("groups", "img"), None, ("head", "rep"))
    return jax.shard_map(body, mesh=mesh, in_specs=in_specs, out_specs=out_specs, check_vma=False)
```

```python
import functools
import math

import jax
import jax.numpy as jnp
from jax import lax
from jax.experimental import pallas as pl
from jax.experimental.pallas import tpu as pltpu
from jax.sharding import PartitionSpec as P

HEAD_DIM = 64
NORM_EPSILON = 1e-06
LANES = 128
SPAN_PARTS = (1,) * 9
GROUPS = (5, 7, 9)
QUOTA = 2
AHEAD = 2
UNROLL = 3
VALUE_SCALE = 512.0
QUERY_SCALE = HEAD_DIM**-0.5 * math.log2(math.e)


def dot(left_side, right_side):
    return jnp.dot(left_side, right_side, preferred_element_type=jnp.float32)


def dot_nt(left_side, right_side):
    return lax.dot_general(
        left_side, right_side, (((1,), (1,)), ((), ())), preferred_element_type=jnp.float32
    )


def project_rows(rows, gq, gk, wq_ref, wk_ref, wv_ref):
    widened = rows.astype(jnp.float32)
    center = widened - jnp.mean(widened, axis=-1, keepdims=True)
    spread = jnp.mean(center * center, axis=-1, keepdims=True)
    base = center * lax.rsqrt(spread + NORM_EPSILON)
    query_in = (base * gq).astype(jnp.bfloat16)
    key_in = (base * gk).astype(jnp.bfloat16)
    queries = (dot(query_in, wq_ref[...]) * QUERY_SCALE).astype(jnp.bfloat16)
    keys = dot(key_in, wk_ref[...]).astype(jnp.bfloat16)
    values = (dot(key_in, wv_ref[...]) * (1.0 / VALUE_SCALE)).astype(jnp.bfloat16)
    return queries, keys, values


def decode_kernel(
    x_ref, wq_ref, wk_ref, wv_ref, wo_ref, wh_ref, gq_ref, gk_ref, out_ref, q_ref, k_ref, v_ref, att_ref
):
    tokens, width = x_ref.shape[1:]
    half = tokens // 2
    gq, gk = gq_ref[...], gk_ref[...]

    @pl.loop(0, 4)
    def _(step):
        side = step // 2
        rows = pl.ds(pl.multiple_of((step % 2) * half, half), half)
        queries, keys, values = project_rows(
            x_ref[side, rows, :], gq, gk, wq_ref, wk_ref, wv_ref
        )
        q_ref[side, rows, :] = queries
        k_ref[side, rows, :] = keys
        v_ref[side, rows, :] = values

    blocks = width // LANES

    @pl.loop(0, 2 * blocks)
    def _(step):
        side = step // blocks
        cols = pl.ds(pl.multiple_of(step % blocks * LANES, LANES), LANES)
        att_ref[side, :, cols] = attend_block(
            q_ref[side, :, cols], k_ref[1 - side, :, cols], v_ref[1 - side, :, cols]
        )

    @pl.loop(0, 2)
    def _(side):
        out_ref[side] = finish(x_ref[side], att_ref[side], wo_ref, wh_ref[...], out_ref.shape[1])


def decode(x, wq, wk, wv, wo, wht, gq, gk, channels):
    tokens, width = x.shape[1:]
    scratch = pltpu.VMEM((2, tokens, width), jnp.bfloat16)
    return pl.pallas_call(
        decode_kernel,
        out_shape=jax.ShapeDtypeStruct((2, channels, tokens), jnp.float32),
        scratch_shapes=[scratch] * 4,
        compiler_params=pltpu.CompilerParams(vmem_limit_bytes=48 * 2**20),
        name="decode",
    )(x, wq, wk, wv, wo, wht, gq, gk)


def attend_block(q, k, v):
    lane = lax.broadcasted_iota(jnp.int32, q.shape, 1)
    out = None
    for sub in range(LANES // HEAD_DIM):
        mine = (lane >= sub * HEAD_DIM) & (lane < (sub + 1) * HEAD_DIM)
        scores = dot_nt(jnp.where(mine, q, jnp.zeros_like(q)), k)
        weights = jnp.exp2(scores)
        inverse = 1.0 / jnp.sum(weights, axis=1, keepdims=True)
        probabilities = (weights * inverse).astype(jnp.bfloat16)
        part = dot(probabilities, v) * VALUE_SCALE
        out = part if out is None else jnp.where(mine, part, out)
    return out.astype(jnp.bfloat16)


def finish(own, attended, wo_ref, wh_rows, channels):
    residual = (own.astype(jnp.float32) + dot(attended, wo_ref[...])).astype(jnp.bfloat16)
    decoded = dot_nt(wh_rows, residual)
    last = decoded[channels - 1 : channels]
    confidence = 1.0 + jnp.maximum(last, 0.0) + jnp.log1p(jnp.exp(-jnp.abs(last)))
    row = lax.broadcasted_iota(jnp.int32, (channels, decoded.shape[1]), 0)
    return jnp.where(row == channels - 1, confidence, decoded[:channels] * confidence)


def fused_kernel(
    sizes, spans, pairs_hbm, enc_hbm, we_hbm, wq_hbm, wk_hbm, wv_hbm, wo_hbm, wh_hbm, gq_hbm, gk_hbm, out_ref,
    enc_ref, we_ref, wq_ref, wk_ref, wv_ref, wo_ref, send_ref, land_refs, xs_refs, xr_refs,
    emb_ref, q_ref, k_ref, v_ref, att_ref, sum_ref, view_ref, part_ref, back_ref, wh_ref, gq_ref, gk_ref, pairs,
    small_sem, pair_sem, enc_sem, wl_sem, ws_sem, wr_sem, zs_sem, zr_sem, xs_sem, xr_sem, bs_sem, br_sem,
):
    owners, heads, reps = sizes
    i, h, r = lax.axis_index("img"), lax.axis_index("head"), lax.axis_index("rep")
    images, rows = enc_ref.shape[:2]
    width = emb_ref.shape[2]
    blocks = width // LANES
    mesh_ids = pl.DeviceIdType.MESH
    count = owners * heads * reps
    me = (i * heads + h) * reps + r
    peer = (i * heads + (1 - h)) * reps + r

    barrier = pltpu.get_barrier_semaphore()

    neighbours = [{"img": (i + step) % owners} for step in range(1, owners)]
    neighbours += [{"head": 1 - h}, {"rep": 1 - r}]
    for neighbour in neighbours:
        pl.semaphore_signal(barrier, inc=1, device_id=neighbour, device_id_type=mesh_ids)
    pairs_copy = pltpu.make_async_copy(pairs_hbm, pairs, pair_sem)
    pairs_copy.start()
    weights = (
        (we_hbm, we_ref), (wk_hbm, wk_ref), (wv_hbm, wv_ref), (wq_hbm, wq_ref), (wo_hbm, wo_ref)
    )

    def place(n, rep):
        half, full = weights[n]
        depth = half.shape[0]
        return full.at[pl.ds(pl.multiple_of(rep * depth, depth), depth)]

    def weight_local(n):
        return pltpu.make_async_copy(weights[n][0], place(n, r), wl_sem.at[n])

    def weight_remote(n, step):
        return pltpu.make_async_remote_copy(
            src_ref=weights[n][0],
            dst_ref=place(n, r),
            send_sem=ws_sem.at[n, step],
            recv_sem=wr_sem.at[n, step],
            device_id={"rep": (r + step) % reps},
            device_id_type=mesh_ids,
        )

    weight_local(0).start()
    enc_copy = pltpu.make_async_copy(enc_hbm, enc_ref, enc_sem)
    enc_copy.start()
    for n in range(1, 5):
        weight_local(n).start()
    small = [
        pltpu.make_async_copy(source_ref, target_ref, small_sem.at[n])
        for n, (source_ref, target_ref) in enumerate(((wh_hbm, wh_ref), (gq_hbm, gq_ref), (gk_hbm, gk_ref)))
    ]
    for copy in small:
        copy.start()

    pl.semaphore_wait(barrier, len(neighbours))
    for step in range(1, reps):
        weight_remote(0, step).start()

    def weight_wait(n):
        weight_local(n).wait()
        for step in range(1, reps):
            weight_remote(n, step).wait_recv()

    middle = owners // 2
    low = i // middle

    def source(k):
        base = (low + k // middle) % 2 * middle
        return base + (i % middle + k) % middle

    order = list(range(middle, owners)) + list(range(1, middle))

    def z_copy(d, c):
        offset, n = spans[c]
        return pltpu.make_async_remote_copy(
            src_ref=send_ref.at[d, pl.ds(offset, n)],
            dst_ref=land_refs[c].at[i],
            send_sem=zs_sem.at[d, c],
            recv_sem=zr_sem.at[i, c],
            device_id={"img": d},
            device_id_type=mesh_ids,
        )

    def z_arrival(a, c):
        offset, n = spans[c]
        return pltpu.make_async_remote_copy(
            src_ref=send_ref.at[a, pl.ds(offset, n)],
            dst_ref=land_refs[c].at[a],
            send_sem=zs_sem.at[a, c],
            recv_sem=zr_sem.at[a, c],
            device_id={"img": a},
            device_id_type=mesh_ids,
        )

    def x_copy(c):
        return pltpu.make_async_remote_copy(
            src_ref=xs_refs[c],
            dst_ref=xr_refs[c],
            send_sem=xs_sem.at[c],
            recv_sem=xr_sem.at[c],
            device_id={"head": 1 - h},
            device_id_type=mesh_ids,
        )

    pairs_copy.wait()
    enc_copy.wait()
    weight_wait(0)

    def pick_for(d):
        pick = 0
        for head in range(heads):
            for side in range(2):
                image = pairs[side, (d * heads + head) * reps + r]
                pick = pick + jnp.where(image // images == i, image % images, 0)
        return pick

    targets = [source(k) for k in order] + [i]
    picks = [pick_for(d) for d in targets]

    for c, (offset, n) in enumerate(spans):
        stacked = jnp.concatenate([enc_ref[pick, pl.ds(offset, n), :] for pick in picks], axis=0)
        embedded = dot(stacked, we_ref[...]).astype(jnp.bfloat16)
        for k, d in enumerate(targets):
            mine = embedded[k * n : (k + 1) * n]
            if k < owners - 1:
                send_ref[d, pl.ds(offset, n), :] = mine
                if c < AHEAD:
                    z_copy(d, c).start()
            else:
                land_refs[c][i] = mine
        if c == 0:
            for w in range(1, 5):
                for step in range(1, reps):
                    weight_remote(w, step).start()

    lane = lax.broadcasted_iota(jnp.int32, (1, LANES), 1)
    first = lane < HEAD_DIM
    for offset, n in spans:
        for sub in range(2):
            ones = jnp.where(first == (sub == 0), 1.0, 0.0).astype(jnp.bfloat16)
            v_ref[:, :, pl.ds(4 * offset + 2 * n * sub, 2 * n), pl.ds(LANES, LANES)] = jnp.broadcast_to(
                ones[None, None], (2, blocks, 2 * n, LANES)
            )

    own = [pairs[side, me] // images for side in range(2)]
    other = [pairs[side, peer] // images for side in range(2)]
    for n in range(1, 4):
        weight_wait(n)
    for copy in small:
        copy.wait()
    gq, gk = gq_ref[...][None], gk_ref[...][None]
    zero = jnp.zeros((), jnp.bfloat16)

    def near_rows(c):
        offset, n = spans[c]
        return pl.ds(pl.multiple_of(h * rows + offset, 16), n)

    def far_rows(c):
        offset, n = spans[c]
        return pl.ds(pl.multiple_of((1 - h) * rows + offset, 16), n)

    def forward(c):
        for k in order:
            z_arrival(source(k), c).wait_recv()
        if c + AHEAD < len(spans):
            for k in order:
                z_copy(source(k), c + AHEAD).start()
        for side in range(2):
            xs_refs[c][side] = land_refs[c][other[side]]
        x_copy(c).start()

    def project(c):
        offset, n = spans[c]
        x_copy(c).wait_recv()
        parts = []
        for side in range(2):
            parts += [land_refs[c][own[side]], xr_refs[c][side]]
        for side in range(2):
            emb_ref[side, near_rows(c), :] = parts[2 * side]
            emb_ref[side, far_rows(c), :] = parts[2 * side + 1]
        queries, keys, values = project_rows(
            jnp.concatenate(parts, axis=0), gq, gk, wq_ref, wk_ref, wv_ref
        )
        for side in range(2):
            top = 2 * side * n
            q_ref[side, near_rows(c), :] = queries[top : top + n]
            q_ref[side, far_rows(c), :] = queries[top + n : top + 2 * n]
            for blk in range(blocks):
                cols = slice(blk * LANES, (blk + 1) * LANES)
                key, value = keys[top : top + 2 * n, cols], values[top : top + 2 * n, cols]
                doubled = jnp.concatenate(
                    [jnp.where(first, key, zero), jnp.where(first, zero, key)], axis=0
                )
                k_ref[side, blk, :, pl.ds(4 * offset, 4 * n)] = doubled.T
                for sub in range(2):
                    span = pl.ds(4 * offset + 2 * n * sub, 2 * n)
                    keep = first == (sub == 0)
                    v_ref[side, blk, span, pl.ds(0, LANES)] = jnp.where(keep, value, zero)

    def attend(steps, begin, end):
        @pl.loop(begin, end)
        def _(t):
            items = []
            for u in range(UNROLL):
                place = t * UNROLL + u
                for step in steps:
                    items.append((place // blocks, place % blocks, step))

            def lanes(blk):
                return pl.ds(pl.multiple_of(blk * LANES, LANES), LANES)

            def score(item):
                side, blk, (pieces, keys, _, _) = item
                queries = [q_ref[side, pl.ds(start, n), lanes(blk)] for start, n in pieces]
                joined = queries[0] if len(queries) == 1 else jnp.concatenate(queries, axis=0)
                return dot(joined, k_ref[1 - side, blk, :, keys])

            scores = score(items[0])
            for place, item in enumerate(items):
                later = score(items[place + 1]) if place + 1 < len(items) else None
                side, blk, (pieces, keys, adds, ends) = item
                sums = dot(jnp.exp2(scores).astype(jnp.bfloat16), v_ref[1 - side, blk, keys])
                top = 0
                for start, n in pieces:
                    rows_here = pl.ds(start, n)
                    mine = sums[top : top + n]
                    top += n
                    if adds:
                        mine = mine + sum_ref[side, blk, rows_here]
                    if ends:
                        att_ref[side, rows_here, lanes(blk)] = (
                            mine[:, :LANES] * (1.0 / mine[:, LANES:]) * VALUE_SCALE
                        ).astype(jnp.bfloat16)
                    else:
                        sum_ref[side, blk, rows_here] = mine
                scores = later

    def old_steps(g):
        low_row, high_row = edges[g], edges[g + 1]
        ends = g == len(GROUPS) - 1
        return [
            (((head * rows, low_row),), pl.ds(4 * low_row, 4 * (high_row - low_row)), True, ends)
            for head in range(heads)
        ]

    def new_steps(g):
        low_row, high_row = edges[g], edges[g + 1]
        ends = g == len(GROUPS) - 1
        pieces = tuple((head * rows + low_row, high_row - low_row) for head in range(heads))
        if high_row - low_row > 128:
            return [((piece,), pl.ds(0, 4 * high_row), False, ends) for piece in pieces]
        return [(pieces, pl.ds(0, 4 * high_row), False, ends)]

    last = len(spans) - 1
    edges = [0] + [sum(spans[g - 1]) for g in GROUPS]
    turns = 2 * blocks // UNROLL
    ready = []
    for c in range(last + 1):
        forward(c)
        if c > 0:
            project(c - 1)
        if c in GROUPS:
            g = GROUPS.index(c)
            ready += [((old_steps(g) if g else []) + new_steps(g), turn) for turn in range(turns)]
        for steps, turn in ready[:QUOTA]:
            attend(steps, turn, turn + 1)
        ready = ready[QUOTA:]
    for steps, turn in ready:
        attend(steps, turn, turn + 1)
    project(last)
    attend(old_steps(len(GROUPS) - 1) + new_steps(len(GROUPS) - 1), 0, turns)

    weight_wait(4)
    shares = heads * reps
    channels = out_ref.shape[0] + 1
    part = out_ref.shape[2]
    wh_rows = wh_ref[...]
    extra = part - LANES
    strips = channels // 4
    order_rows = [(share * part, LANES) for share in range(shares)]
    order_rows += [(share * part + LANES, extra) for share in range(shares)]

    def arrange(ref, side):
        return jnp.concatenate([ref[side, pl.ds(start, n), :] for start, n in order_rows], axis=0)

    for side in range(2):
        weighted = finish(arrange(emb_ref, side), arrange(att_ref, side), wo_ref, wh_rows, channels)
        for share in range(shares):
            left = shares * LANES + share * extra
            strip = [weighted[4 * g : 4 * g + 4, left : left + extra] for g in range(strips)]
            strip.append(jnp.zeros((4, LANES - strips * extra), jnp.float32))
            packed = jnp.concatenate(
                [weighted[:, share * LANES : (share + 1) * LANES], jnp.concatenate(strip, axis=1)], axis=0
            )
            view_ref[side, share] = packed.astype(view_ref.dtype)

    def b_copy(target):
        return pltpu.make_async_remote_copy(
            src_ref=part_ref.at[target],
            dst_ref=back_ref.at[me],
            send_sem=bs_sem.at[target],
            recv_sem=br_sem.at[me],
            device_id={
                "img": target // shares,
                "head": target // reps % heads,
                "rep": target % reps,
            },
            device_id_type=mesh_ids,
        )

    def b_arrival(src):
        return pltpu.make_async_remote_copy(
            src_ref=part_ref.at[src],
            dst_ref=back_ref.at[src],
            send_sem=bs_sem.at[src],
            recv_sem=br_sem.at[src],
            device_id={"img": src // shares, "head": src // reps % heads, "rep": src % reps},
            device_id_type=mesh_ids,
        )

    mine_share = h * reps + r
    for d in [source(k) for k in order]:
        side = jnp.where(own[0] == d, 0, 1)
        for share in range(shares):
            part_ref[d * shares + share] = view_ref[side, share]
            b_copy(d * shares + share).start()
    near_side = jnp.where(own[0] == i, 0, 1)
    for step in range(1, shares):
        share = (mine_share + step) % shares
        part_ref[i * shares + share] = view_ref[near_side, share]
        b_copy(i * shares + share).start()
    back_ref[me] = view_ref[near_side, mine_share]

    for c in range(last + 1):
        for k in order:
            z_copy(source(k), c).wait_send()
        x_copy(c).wait_send()
    for n in range(5):
        for step in range(1, reps):
            weight_remote(n, step).wait_send()

    for step in range(1, count):
        b_arrival((me + step) % count).wait_recv()

    totals = [jnp.zeros(back_ref.shape[1:], jnp.float32) for _ in range(images)]
    for src in range(count):
        one, two = pairs[0, src], pairs[1, src]
        local = jnp.where(
            one // images == i,
            one % images,
            jnp.where(two // images == i, two % images, images),
        )
        block = back_ref[src].astype(jnp.float32)
        for image in range(images):
            totals[image] = totals[image] + jnp.where(local == image, block, 0.0)
    for image in range(images):
        packed = totals[image]
        rest = [packed[channels:, g * extra : (g + 1) * extra] for g in range(strips)]
        total = jnp.concatenate([packed[:channels], jnp.concatenate(rest, axis=0)], axis=1)
        out_ref[:, image, :] = total[: channels - 1] / jnp.maximum(total[channels - 1 :], 1.0)

    for step in range(1, count):
        b_copy((me + step) % count).wait_send()


def fused(enc, pairs, w_embed, w_query, w_key, w_value, w_out, wht, gq, gk, spans):
    owners, heads, reps = (lax.axis_size(name) for name in ("img", "head", "rep"))
    images, rows, enc_width = enc.shape
    width = w_embed.shape[1]
    tokens = heads * rows
    part = rows // reps
    channels = wht.shape[0]
    count = owners * heads * reps
    blocks = width // LANES
    bf16 = jnp.bfloat16
    dma = pltpu.SemaphoreType.DMA
    full = pltpu.VMEM((width, width), bf16)
    any_space = pl.BlockSpec(memory_space=pl.ANY)
    vmem = pl.BlockSpec(memory_space=pltpu.VMEM)
    pieces = len(spans)
    return pl.pallas_call(
        functools.partial(fused_kernel, (owners, heads, reps), spans),
        out_shape=jax.ShapeDtypeStruct((channels - 1, images, part), jnp.float32),
        in_specs=[any_space] * 10,
        out_specs=vmem,
        scratch_shapes=[
            pltpu.VMEM(enc.shape, bf16),
            pltpu.VMEM((enc_width, width), bf16),
            full, full, full, full,
            pltpu.VMEM((owners, rows, width), bf16),
            tuple(pltpu.VMEM((owners, n, width), bf16) for _, n in spans),
            tuple(pltpu.VMEM((2, n, width), bf16) for _, n in spans),
            tuple(pltpu.VMEM((2, n, width), bf16) for _, n in spans),
            pltpu.VMEM((2, tokens, width), bf16),
            pltpu.VMEM((2, tokens, width), bf16),
            pltpu.VMEM((2, blocks, LANES, 2 * tokens), bf16),
            pltpu.VMEM((2, blocks, 2 * tokens, 2 * LANES), bf16),
            pltpu.VMEM((2, tokens, width), bf16),
            pltpu.VMEM((2, blocks, tokens, 2 * LANES), jnp.float32),
            pltpu.VMEM((2, heads * reps, channels + 4, LANES), bf16),
            pltpu.VMEM((count, channels + 4, LANES), bf16),
            pltpu.VMEM((count, channels + 4, LANES), bf16),
            pltpu.VMEM(wht.shape, bf16),
            pltpu.VMEM(gq.shape, jnp.float32),
            pltpu.VMEM(gk.shape, jnp.float32),
            pltpu.SMEM(pairs.shape, jnp.int32),
            dma((3,)),
            dma(()),
            dma(()),
            dma((5,)),
            dma((5, reps)),
            dma((5, reps)),
            dma((owners, pieces)),
            dma((owners, pieces)),
            dma((pieces,)),
            dma((pieces,)),
            dma((count,)),
            dma((count,)),
        ],
        compiler_params=pltpu.CompilerParams(
            collective_id=0, has_side_effects=True, vmem_limit_bytes=56 * 2**20
        ),
        name="decode_views",
    )(pairs, enc, w_embed, w_query, w_key, w_value, w_out, wht, gq, gk).transpose(1, 0, 2)


def cut(rows):
    unit = rows // 9
    spans, offset = [], 0
    for parts in SPAN_PARTS:
        spans.append((offset, parts * unit))
        offset += parts * unit
    return tuple(spans)


def take_each(array, index):
    return jnp.stack(
        [lax.dynamic_index_in_dim(array, index[k], 0, keepdims=False) for k in range(index.shape[0])]
    )


def body(enc, pair_list, w_embed, w_query, w_key, w_value, w_out, w_head, gain_query, gain_key):
    owner_count = lax.axis_size("img")
    head_count = lax.axis_size("head")
    rep_count = lax.axis_size("rep")
    my_owner = lax.axis_index("img")
    my_rep = lax.axis_index("rep")
    img_count, row_count, enc_width = enc.shape
    slot_count = 2 * head_count
    assert slot_count == owner_count
    channels = w_head.shape[1]
    extra = row_count // rep_count - LANES
    fits = 0 < extra and extra % 16 == 0 and channels % 4 == 0 and channels // 4 * extra < LANES
    if fits and head_count == 2 and rep_count == 2 and row_count % 144 == 0 and owner_count % 2 == 0:
        return fused(
            enc, pair_list.T, w_embed, w_query, w_key, w_value, w_out, w_head.T,
            gain_query, gain_key, cut(row_count),
        )
    wht = jnp.pad(w_head.T, ((0, -channels % 16), (0, 0)))
    full_embed, full_query, full_key, full_value, full_out = (
        lax.all_gather(w, "rep", axis=0, tiled=True)
        for w in (w_embed, w_query, w_key, w_value, w_out)
    )
    layout = lax.dynamic_index_in_dim(
        pair_list.reshape(owner_count, head_count, rep_count, 2), my_rep, 2, keepdims=False
    ).reshape(owner_count, slot_count)
    slot_owner = layout // img_count
    mine = slot_owner == my_owner
    pick = jnp.sum(jnp.where(mine, layout % img_count, 0), axis=1)
    group_owner = lax.dynamic_index_in_dim(slot_owner, my_owner, 0, keepdims=False)
    owner_index = group_owner.reshape(head_count, 2).T.reshape(-1)
    slot_of = jnp.sum(
        jnp.where(group_owner[None, :] == jnp.arange(slot_count)[:, None], jnp.arange(slot_count)[None, :], 0),
        axis=1,
    )

    rows = take_each(enc, pick).reshape(-1, enc_width)
    embedded = dot(rows, full_embed).astype(jnp.bfloat16).reshape(owner_count, row_count, -1)
    arrived = lax.all_to_all(embedded, "img", split_axis=0, concat_axis=0, tiled=True)
    grouped = take_each(arrived, owner_index).reshape(2, head_count, row_count, -1)
    spread = lax.all_to_all(grouped, "head", split_axis=1, concat_axis=1, tiled=True)
    x = spread.reshape(2, head_count * row_count, spread.shape[-1])
    weighted = decode(
        x, full_query, full_key, full_value, full_out, wht, gain_query[None], gain_key[None], channels
    )
    back = lax.all_to_all(
        weighted.reshape(2, channels, head_count, row_count),
        "head",
        split_axis=2,
        concat_axis=2,
        tiled=True,
    )
    by_slot = back.transpose(2, 0, 1, 3).reshape(slot_count, channels, row_count)
    received = lax.all_to_all(take_each(by_slot, slot_of), "img", split_axis=0, concat_axis=0, tiled=True)
    chosen = (pick[:, None] == jnp.arange(img_count)[None, :]).astype(jnp.float32)
    totals = jnp.einsum("qi,qxr->ixr", chosen, received, precision=lax.Precision.HIGHEST)
    shares = lax.psum_scatter(totals, "rep", scatter_dimension=2, tiled=True)
    return shares[:, :-1] / jnp.maximum(shares[:, -1:], 1.0)


def solution(mesh):
    in_specs = (
        P(("groups", "img"), "head", None),
        P("groups", None),
        P("rep", None),
        P("rep", None),
        P("rep", None),
        P("rep", None),
        P("rep", None),
        P(),
        P(),
        P(),
    )
    out_specs = P(("groups", "img"), None, ("head", "rep"))
    return jax.shard_map(body, mesh=mesh, in_specs=in_specs, out_specs=out_specs, check_vma=False)
```
